32 devices in a mesh: grp: 4 (over x, core), wide: 8 (over z, y).
Axes of the slice: x: 2, y: 2, z: 4, core: 2. Of those that a mesh axis runs over, the one named last changes fastest.
Arguments:
- expression: float32 [1024, 4096], P(('grp', 'wide'))
- assignment: int32 [16], replicated, may hold values from 0 to 15, each once
- pairing: int32 [2, 16], replicated, may hold values from 0 to 15, as said below
Outputs:
- cross_scores: float32 [2, 16, 256, 256], P(None, 'wide', 'grp')
The draws below stay inside these ranges and needn't reach their ends.
Inputs may be any that keep to these rules, and one draw needn't show every extreme that they name: Row r of pairing is round r of one round-robin plan over the 16 panels: every panel has a partner other than itself, and the partner's partner is the panel.
All inputs are finite; a program needn't handle non-finite values.
Results may differ from the reference program's by a relative error of at most 0.0043.
Values may be sent and summed in bfloat16 or wider, within the bound.
No kernel may reach another device: no remote copies, remote signals or barrier semaphores. Data moves between devices by JAX's collectives and lax.ppermute only.
A program may use at most 192 MiB of HBM per device.

```python
import math
import jax
import jax.numpy as jnp
from jax import lax

PANEL = 256
ROUNDS = 2
PANELS = 16
GENES = 4096
CELLS = 1024


def draw_expression(key, part):
    keys = [jax.random.fold_in(key, 11 + i) for i in range(7)]
    where = jnp.arange(CELLS, dtype=jnp.float32)[:, None] / (CELLS - 1)
    row_scale = jnp.exp(jax.random.uniform(keys[0], (CELLS, 1), jnp.float32, 0.0, math.log(10.0))) * jnp.exp(where * math.log(3.0))
    col_scale = jnp.exp(jax.random.uniform(keys[1], (1, GENES), jnp.float32, 0.0, math.log(10.0)))
    offset = jax.random.uniform(keys[2], (1, GENES), jnp.float32, 0.0, 3.0) * col_scale
    noise = jax.random.normal(keys[3], (CELLS, GENES), jnp.float32)
    return (offset + row_scale * col_scale * noise).astype(jnp.float32)


def draw_pairing(key, part):
    span = PANELS - 1
    order = jax.random.permutation(jax.random.fold_in(key, 101), PANELS)
    picked = jax.random.permutation(jax.random.fold_in(key, 102), span)[:ROUNDS]
    spots = jnp.arange(PANELS, dtype=jnp.int32)

    def one_round(rnd):
        rnd = rnd.astype(jnp.int32)
        other = jnp.mod(2 * rnd - spots, span)
        other = jnp.where(other == spots, span, other)
        other = jnp.where(spots == span, rnd, other)
        return jnp.zeros((PANELS,), jnp.int32).at[order].set(order[other].astype(jnp.int32))
    return jax.vmap(one_round)(picked).astype(jnp.int32)


def setup_inputs(seed: int = 0) -> dict:
    key_list = jax.random.split(jax.random.key(seed), 4)
    return {
        "expression": draw_expression(jax.random.fold_in(key_list[3], 71), 0),
        "assignment": jax.random.permutation(key_list[1], PANELS).astype(jnp.int32),
        "pairing": draw_pairing(jax.random.fold_in(key_list[3], 71), 0),
    }


def reference(expression, assignment, pairing):
    mean = lax.optimization_barrier(jnp.sum(expression, axis=0)) / CELLS
    var = lax.optimization_barrier(jnp.sum(expression * expression, axis=0)) / CELLS - mean * mean
    scaled = ((expression - mean) * lax.rsqrt(var + 1e-05)).astype(jnp.bfloat16)

    def one_tile(pair):
        first = lax.dynamic_slice_in_dim(scaled, (pair[0] * PANEL).astype(jnp.int32), PANEL, 1)
        second = lax.dynamic_slice_in_dim(scaled, (pair[1] * PANEL).astype(jnp.int32), PANEL, 1)
        return jnp.dot(first.T, second, preferred_element_type=jnp.float32)
    tiles = []
    for rnd in range(ROUNDS):
        partner = pairing[rnd][assignment]
        tiles.append(lax.map(one_tile, (assignment, partner)))
    return jnp.stack(tiles, axis=0) * CELLS ** (-0.5)
```

```python
import functools

import jax
import jax.numpy as jnp
from jax import lax
from jax.experimental import pallas as pl
from jax.experimental.pallas import tpu as pltpu
from jax.sharding import PartitionSpec as P

SLOTS = 2
ROUNDS = 2
PICKED = SLOTS * (1 + ROUNDS)
SIDE = 16
F32 = jnp.float32
BF16 = jnp.bfloat16


def split_two(value):
    high = value.astype(BF16).astype(F32)
    return high, value - high


def prep_kernel(assignment, pairing, x_ref, out_ref, centred, high_rows, low_rows, side):
    cells, genes = x_ref.shape
    panels = assignment.shape[0]
    panel = genes // panels
    n_wide = out_ref.shape[0]

    def one_panel(p, carry):
        start = pl.multiple_of(p * panel, panel)
        block = x_ref[:, pl.ds(start, panel)]
        mean = jnp.sum(block, axis=0, keepdims=True) * (1.0 / cells)
        high, rest = split_two(mean)
        low = rest.astype(BF16).astype(F32)
        centred[p] = (block - (high + low)).astype(BF16)
        high_rows[pl.ds(p, 1), :] = high
        low_rows[pl.ds(p, 1), :] = low
        return carry

    lax.fori_loop(0, panels, one_panel, 0, unroll=panels <= 16)
    side[...] = jnp.zeros_like(side)

    def one_message(w, carry):
        for s in range(SLOTS):
            own = assignment[w * SLOTS + s]
            for k in range(1 + ROUNDS):
                p = own if k == 0 else pairing[k - 1, own]
                j = s if k == 0 else SLOTS + s * ROUNDS + k - 1
                out_ref[w, pl.ds(j * cells, cells), :] = centred[p]
                side[pl.ds(j, 1), :] = high_rows[pl.ds(p, 1), :]
                side[pl.ds(PICKED + j, 1), :] = low_rows[pl.ds(p, 1), :]
        out_ref[w, pl.ds(PICKED * cells, SIDE), :] = side[...].astype(BF16)
        return carry

    lax.fori_loop(0, n_wide, one_message, 0, unroll=n_wide <= 8)


def gram_kernel(cells, panel, place, here_ref, there_ref, near_ref, far_ref, stat_ref, tile):
    n_wide = here_ref.shape[0]
    blocks = 2 * n_wide
    rows = blocks * cells
    quarter = panel // 4

    def part(start, size):
        halves = [r[:, pl.ds(start, size), :].reshape(n_wide * size, panel) for r in (here_ref, there_ref)]
        return jnp.concatenate(halves, axis=0)

    member = lax.broadcasted_iota(jnp.int32, (blocks, rows), 1) // cells
    member = (member == lax.broadcasted_iota(jnp.int32, (blocks, rows), 0)).astype(BF16)
    side = jnp.concatenate(
        [r[:, pl.ds(PICKED * cells, SIDE), :].astype(F32) for r in (here_ref, there_ref)], axis=0
    )
    left, right, means, squares = [], [], [], []
    for j in range(PICKED):
        data = part(j * cells, cells)
        sums = jnp.dot(member, data, preferred_element_type=F32)
        block_mean = side[:, j, :] + side[:, PICKED + j, :] + sums * (1.0 / cells)
        mean = jnp.sum(block_mean, axis=0, keepdims=True) * (1.0 / blocks)
        shift = block_mean - mean
        wide_data = data.astype(F32)
        square = jnp.sum(wide_data * wide_data, axis=0, keepdims=True) + jnp.sum(
            cells * (shift * shift) - sums * sums * (1.0 / cells), axis=0, keepdims=True
        )
        means.append(mean)
        squares.append(square)
        high, low = split_two(shift)
        scale = cells // 8
        if j < SLOTS:
            extra = [8.0 * high, 8.0 * low, 8.0 * high, sums * 0.125]
        else:
            extra = [scale * high, scale * high, scale * low, sums * (-8.0 / cells)]
        (left if j < SLOTS else right).append(
            jnp.concatenate([data, jnp.concatenate(extra, axis=0).astype(BF16)], axis=0)
        )
    stats = jnp.concatenate(means + squares + [jnp.zeros((SIDE - 2 * PICKED, panel), F32)], axis=0)
    stat_ref[...] = stats
    mine = place[0]
    near = pl.multiple_of(mine * quarter, quarter)
    far = pl.multiple_of(((mine + 2) % 4) * quarter, quarter)
    for s in range(SLOTS):
        for r in range(ROUNDS):
            t = s * ROUNDS + r
            tile[...] = lax.dot_general(
                left[s], right[t], (((0,), (0,)), ((), ())), preferred_element_type=F32
            )
            near_ref[pl.ds(t * quarter, quarter), :] = tile[pl.ds(near, quarter), :]
            far_ref[pl.ds(t * quarter, quarter), :] = tile[pl.ds(far, quarter), :].astype(BF16)
    high, rest = split_two(stats)
    middle, low = split_two(rest)
    base = SLOTS * ROUNDS * quarter
    for i, value in enumerate((high, middle, low)):
        far_ref[pl.ds(base + i * SIDE, SIDE), :] = value.astype(BF16)


def finish_kernel(total, panel, place, near_ref, far_ref, stat_ref, out_ref, columns):
    quarter = panel // 4
    base = SLOTS * ROUNDS * quarter
    other = sum(far_ref[pl.ds(base + i * SIDE, SIDE), :].astype(F32) for i in (2, 1, 0))
    stats = stat_ref[...]
    both = stats + other
    gap = (stats - other)[0:8]
    var = (both[PICKED : PICKED + 8] * (1.0 / total)) + (gap * gap) * 0.25
    inv = lax.rsqrt(var + 1e-05)
    columns[...] = jnp.concatenate([gap, inv], axis=0).T
    mine = pl.multiple_of(place[0] * quarter, quarter)
    side = columns[pl.ds(mine, quarter), :]
    for s in range(SLOTS):
        gap_row = side[:, s : s + 1]
        inv_row = side[:, 8 + s : 9 + s] * total ** (-0.5)
        for r in range(ROUNDS):
            t = s * ROUNDS + r
            j = SLOTS + t
            rows = pl.ds(t * quarter, quarter)
            tile = near_ref[rows, :] + far_ref[rows, :].astype(F32)
            tile = tile + gap_row * (gap[j : j + 1] * (total / 4))
            out_ref[r, s] = tile * inv_row * inv[j : j + 1]


def shards(expression, assignment, pairing):
    n_wide = lax.axis_size("wide")
    n_grp = lax.axis_size("grp")
    cells, genes = expression.shape
    panel = genes // assignment.shape[0]
    panels = assignment.shape[0]
    quarter = panel // n_grp
    total = cells * n_wide * n_grp
    place = lax.axis_index("grp").reshape(1).astype(jnp.int32)
    smem = pl.BlockSpec(memory_space=pltpu.SMEM)
    vmem = pl.BlockSpec(memory_space=pltpu.VMEM)
    message = PICKED * cells + SIDE
    sent = pl.pallas_call(
        prep_kernel,
        out_shape=jax.ShapeDtypeStruct((n_wide, message, panel), BF16),
        in_specs=[smem, smem, vmem],
        out_specs=vmem,
        scratch_shapes=[
            pltpu.VMEM((panels, cells, panel), BF16),
            pltpu.VMEM((panels, panel), F32),
            pltpu.VMEM((panels, panel), F32),
            pltpu.VMEM((SIDE, panel), F32),
        ],
        name="prep",
    )(assignment, pairing, expression)
    here = lax.all_to_all(sent, "wide", split_axis=0, concat_axis=0, tiled=True)
    there = lax.ppermute(here, "grp", [(i, i ^ 1) for i in range(n_grp)])
    tiles = SLOTS * ROUNDS * quarter
    near, far, stats = pl.pallas_call(
        functools.partial(gram_kernel, cells, panel),
        out_shape=(
            jax.ShapeDtypeStruct((tiles, panel), F32),
            jax.ShapeDtypeStruct((tiles + 3 * SIDE, panel), BF16),
            jax.ShapeDtypeStruct((SIDE, panel), F32),
        ),
        in_specs=[smem, vmem, vmem],
        out_specs=(vmem, vmem, vmem),
        scratch_shapes=[pltpu.VMEM((panel, panel), F32)],
        compiler_params=pltpu.CompilerParams(vmem_limit_bytes=60 << 20),
        name="gram",
    )(place, here, there)
    far = lax.ppermute(far, "grp", [(i, i ^ 2) for i in range(n_grp)])
    return pl.pallas_call(
        functools.partial(finish_kernel, total, panel),
        out_shape=jax.ShapeDtypeStruct((ROUNDS, SLOTS, quarter, panel), F32),
        in_specs=[smem, vmem, vmem, vmem],
        out_specs=vmem,
        scratch_shapes=[pltpu.VMEM((panel, 16), F32)],
        name="finish",
    )(place, near, far, stats)


def solution(mesh):
    placed = (P(("grp", "wide"), None), P(), P())
    return jax.shard_map(
        shards, mesh=mesh, in_specs=placed, out_specs=P(None, "wide", "grp", None), check_vma=False
    )
```

```python
import functools

import jax
import jax.numpy as jnp
from jax import lax
from jax.experimental import pallas as pl
from jax.experimental.pallas import tpu as pltpu
from jax.sharding import PartitionSpec as P

SLOTS = 2
ROUNDS = 2
PICKED = SLOTS * (1 + ROUNDS)
SIDE = 16
F32 = jnp.float32
BF16 = jnp.bfloat16


def split_two(value):
    high = value.astype(BF16).astype(F32)
    return high, value - high


def prep_kernel(assignment, pairing, x_ref, out_ref, centred, high_rows, low_rows, side):
    cells, genes = x_ref.shape
    panels = assignment.shape[0]
    panel = genes // panels
    n_wide = out_ref.shape[0]

    def one_panel(p, carry):
        start = pl.multiple_of(p * panel, panel)
        block = x_ref[:, pl.ds(start, panel)]
        mean = jnp.sum(block, axis=0, keepdims=True) * (1.0 / cells)
        high, rest = split_two(mean)
        low = rest.astype(BF16).astype(F32)
        centred[p] = (block - (high + low)).astype(BF16)
        high_rows[pl.ds(p, 1), :] = high
        low_rows[pl.ds(p, 1), :] = low
        return carry

    lax.fori_loop(0, panels, one_panel, 0, unroll=panels <= 16)
    side[...] = jnp.zeros_like(side)

    def one_message(w, carry):
        for s in range(SLOTS):
            own = assignment[w * SLOTS + s]
            for k in range(1 + ROUNDS):
                p = own if k == 0 else pairing[k - 1, own]
                j = s if k == 0 else SLOTS + s * ROUNDS + k - 1
                out_ref[w, pl.ds(j * cells, cells), :] = centred[p]
                side[pl.ds(j, 1), :] = high_rows[pl.ds(p, 1), :]
                side[pl.ds(PICKED + j, 1), :] = low_rows[pl.ds(p, 1), :]
        out_ref[w, pl.ds(PICKED * cells, SIDE), :] = side[...].astype(BF16)
        return carry

    lax.fori_loop(0, n_wide, one_message, 0, unroll=n_wide <= 8)


def gram_kernel(cells, panel, place, here_ref, there_ref, near_ref, far_ref, stat_ref, tile):
    n_wide = here_ref.shape[0]
    blocks = 2 * n_wide
    rows = blocks * cells
    quarter = panel // 4

    def part(start, size):
        halves = [r[:, pl.ds(start, size), :].reshape(n_wide * size, panel) for r in (here_ref, there_ref)]
        return jnp.concatenate(halves, axis=0)

    member = lax.broadcasted_iota(jnp.int32, (blocks, rows), 1) // cells
    member = (member == lax.broadcasted_iota(jnp.int32, (blocks, rows), 0)).astype(BF16)
    side = jnp.concatenate(
        [r[:, pl.ds(PICKED * cells, SIDE), :].astype(F32) for r in (here_ref, there_ref)], axis=0
    )
    left, right, means, squares = [], [], [], []
    for j in range(PICKED):
        data = part(j * cells, cells)
        sums = jnp.dot(member, data, preferred_element_type=F32)
        block_mean = side[:, j, :] + side[:, PICKED + j, :] + sums * (1.0 / cells)
        mean = jnp.sum(block_mean, axis=0, keepdims=True) * (1.0 / blocks)
        shift = block_mean - mean
        wide_data = data.astype(F32)
        square = jnp.sum(wide_data * wide_data, axis=0, keepdims=True) + jnp.sum(
            cells * (shift * shift) - sums * sums * (1.0 / cells), axis=0, keepdims=True
        )
        means.append(mean)
        squares.append(square)
        high, low = split_two(shift)
        scale = cells // 8
        if j < SLOTS:
            extra = [8.0 * high, 8.0 * low, 8.0 * high, sums * 0.125]
        else:
            extra = [scale * high, scale * high, scale * low, sums * (-8.0 / cells)]
        (left if j < SLOTS else right).append(
            jnp.concatenate([data, jnp.concatenate(extra, axis=0).astype(BF16)], axis=0)
        )
    stats = jnp.concatenate(means + squares + [jnp.zeros((SIDE - 2 * PICKED, panel), F32)], axis=0)
    stat_ref[...] = stats
    mine = place[0]
    near = pl.multiple_of(mine * quarter, quarter)
    far = pl.multiple_of(((mine + 2) % 4) * quarter, quarter)
    for s in range(SLOTS):
        for r in range(ROUNDS):
            t = s * ROUNDS + r
            tile[...] = lax.dot_general(
                left[s], right[t], (((0,), (0,)), ((), ())), preferred_element_type=F32
            )
            near_ref[pl.ds(t * quarter, quarter), :] = tile[pl.ds(near, quarter), :]
            far_ref[pl.ds(t * quarter, quarter), :] = tile[pl.ds(far, quarter), :].astype(BF16)
    high, rest = split_two(stats)
    middle, low = split_two(rest)
    base = SLOTS * ROUNDS * quarter
    for i, value in enumerate((high, middle, low)):
        far_ref[pl.ds(base + i * SIDE, SIDE), :] = value.astype(BF16)


def finish_kernel(total, panel, place, near_ref, far_ref, stat_ref, out_ref, columns):
    quarter = panel // 4
    base = SLOTS * ROUNDS * quarter
    other = sum(far_ref[pl.ds(base + i * SIDE, SIDE), :].astype(F32) for i in (2, 1, 0))
    stats = stat_ref[...]
    both = stats + other
    gap = (stats - other)[0:8]
    var = (both[PICKED : PICKED + 8] * (1.0 / total)) + (gap * gap) * 0.25
    inv = lax.rsqrt(var + 1e-05)
    columns[...] = jnp.concatenate([gap, inv], axis=0).T
    mine = pl.multiple_of(place[0] * quarter, quarter)
    side = columns[pl.ds(mine, quarter), :]
    for s in range(SLOTS):
        gap_row = side[:, s : s + 1]
        inv_row = side[:, 8 + s : 9 + s] * total ** (-0.5)
        for r in range(ROUNDS):
            t = s * ROUNDS + r
            j = SLOTS + t
            rows = pl.ds(t * quarter, quarter)
            tile = near_ref[rows, :] + far_ref[rows, :].astype(F32)
            tile = tile + gap_row * (gap[j : j + 1] * (total / 4))
            out_ref[r, s] = tile * inv_row * inv[j : j + 1]


def on_chip(small):
    if not small:
        return jax.ShapeDtypeStruct, lambda value: value
    return pltpu.VMEM, lambda value: pltpu.with_memory_space_constraint(value, pltpu.VMEM)


def shards(expression, assignment, pairing):
    n_wide = lax.axis_size("wide")
    n_grp = lax.axis_size("grp")
    cells, genes = expression.shape
    panel = genes // assignment.shape[0]
    panels = assignment.shape[0]
    quarter = panel // n_grp
    total = cells * n_wide * n_grp
    place = lax.axis_index("grp").reshape(1).astype(jnp.int32)
    smem = pl.BlockSpec(memory_space=pltpu.SMEM)
    vmem = pl.BlockSpec(memory_space=pltpu.VMEM)
    message = PICKED * cells + SIDE
    received_bytes = 2 * n_wide * message * panel * 2
    array, in_vmem = on_chip(received_bytes <= 4 << 20)
    sent = pl.pallas_call(
        prep_kernel,
        out_shape=array((n_wide, message, panel), BF16),
        in_specs=[smem, smem, vmem],
        out_specs=vmem,
        scratch_shapes=[
            pltpu.VMEM((panels, cells, panel), BF16),
            pltpu.VMEM((panels, panel), F32),
            pltpu.VMEM((panels, panel), F32),
            pltpu.VMEM((SIDE, panel), F32),
        ],
        name="prep",
    )(assignment, pairing, expression)
    here = lax.all_to_all(sent, "wide", split_axis=0, concat_axis=0, tiled=True)
    there = lax.ppermute(here, "grp", [(i, i ^ 1) for i in range(n_grp)])
    tiles = SLOTS * ROUNDS * quarter
    near, far, stats = pl.pallas_call(
        functools.partial(gram_kernel, cells, panel),
        out_shape=(
            array((tiles, panel), F32),
            array((tiles + 3 * SIDE, panel), BF16),
            array((SIDE, panel), F32),
        ),
        in_specs=[smem, vmem, vmem],
        out_specs=(vmem, vmem, vmem),
        scratch_shapes=[pltpu.VMEM((panel, panel), F32)],
        compiler_params=pltpu.CompilerParams(vmem_limit_bytes=min(60 << 20, (8 << 20) + 6 * received_bytes)),
        name="gram",
    )(place, in_vmem(here), in_vmem(there))
    far = lax.ppermute(far, "grp", [(i, i ^ 2) for i in range(n_grp)])
    return pl.pallas_call(
        functools.partial(finish_kernel, total, panel),
        out_shape=jax.ShapeDtypeStruct((ROUNDS, SLOTS, quarter, panel), F32),
        in_specs=[smem, vmem, vmem, vmem],
        out_specs=vmem,
        scratch_shapes=[pltpu.VMEM((panel, 16), F32)],
        name="finish",
    )(place, in_vmem(near), in_vmem(far), in_vmem(stats))


def solution(mesh):
    placed = (P(("grp", "wide"), None), P(), P())
    return jax.shard_map(
        shards, mesh=mesh, in_specs=placed, out_specs=P(None, "wide", "grp", None), check_vma=False
    )
```

```python
import functools

import jax
import jax.numpy as jnp
from jax import lax
from jax.experimental import pallas as pl
from jax.experimental.pallas import tpu as pltpu
from jax.sharding import Mesh
from jax.sharding import PartitionSpec as P

SLOTS = 2
ROUNDS = 2
PICKED = SLOTS * (1 + ROUNDS)
SIDE = 16
STATS = 8
F32 = jnp.float32
BF16 = jnp.bfloat16


def split_two(value):
    high = value.astype(BF16).astype(F32)
    return high, value - high


def prep_kernel(assignment, pairing, x_ref, out_ref, centred, high_rows, low_rows, side):
    cells, genes = x_ref.shape
    panels = assignment.shape[0]
    panel = genes // panels
    n_wide = out_ref.shape[0]

    def one_panel(p, carry):
        start = pl.multiple_of(p * panel, panel)
        block = x_ref[:, pl.ds(start, panel)]
        mean = jnp.sum(block, axis=0, keepdims=True) * (1.0 / cells)
        high, rest = split_two(mean)
        low = rest.astype(BF16).astype(F32)
        centred[p] = (block - (high + low)).astype(BF16)
        high_rows[pl.ds(p, 1), :] = high
        low_rows[pl.ds(p, 1), :] = low
        return carry

    lax.fori_loop(0, panels, one_panel, 0, unroll=panels <= 16)
    side[...] = jnp.zeros_like(side)

    def one_message(w, carry):
        for s in range(SLOTS):
            owner = (w + s * (n_wide // 2)) % n_wide
            own = assignment[owner * SLOTS + s]
            for k in range(1 + ROUNDS):
                p = own if k == 0 else pairing[k - 1, own]
                j = s if k == 0 else SLOTS + s * ROUNDS + k - 1
                out_ref[w, pl.ds(j * cells, cells), :] = centred[p]
                side[pl.ds(j, 1), :] = high_rows[pl.ds(p, 1), :]
                side[pl.ds(PICKED + j, 1), :] = low_rows[pl.ds(p, 1), :]
        out_ref[w, pl.ds(PICKED * cells, SIDE), :] = side[...].astype(BF16)
        return carry

    lax.fori_loop(0, n_wide, one_message, 0, unroll=n_wide <= 8)


def gram_kernel(cells, place, nearer, here_ref, there_ref, keep_ref, x_ref, half_ref, both_ref, tile, stat):
    n_wide, _, panel = here_ref.shape
    blocks = 2 * n_wide
    rows = blocks * cells
    quarter = panel // 4

    def part(start, size):
        halves = [r[:, pl.ds(start, size), :].reshape(n_wide * size, panel) for r in (here_ref, there_ref)]
        return jnp.concatenate(halves, axis=0)

    member = lax.broadcasted_iota(jnp.int32, (blocks, rows), 1) // cells
    member = (member == lax.broadcasted_iota(jnp.int32, (blocks, rows), 0)).astype(BF16)
    side = jnp.concatenate(
        [r[:, pl.ds(PICKED * cells, SIDE), :].astype(F32) for r in (here_ref, there_ref)], axis=0
    )
    left, right, means, squares = [], [], [], []
    for j in range(PICKED):
        data = part(j * cells, cells)
        sums = jnp.dot(member, data, preferred_element_type=F32)
        block_mean = side[:, j, :] + side[:, PICKED + j, :] + sums * (1.0 / cells)
        mean = jnp.sum(block_mean, axis=0, keepdims=True) * (1.0 / blocks)
        shift = block_mean - mean
        wide_data = data.astype(F32)
        square = jnp.sum(wide_data * wide_data, axis=0, keepdims=True) + jnp.sum(
            cells * (shift * shift) - sums * sums * (1.0 / cells), axis=0, keepdims=True
        )
        means.append(mean)
        squares.append(square)
        high, low = split_two(shift)
        scale = cells // 8
        if j < SLOTS:
            extra = [8.0 * high, 8.0 * low, 8.0 * high, sums * 0.125]
        else:
            extra = [scale * high, scale * high, scale * low, sums * (-8.0 / cells)]
        (left if j < SLOTS else right).append(
            jnp.concatenate([data, jnp.concatenate(extra, axis=0).astype(BF16)], axis=0)
        )
    for s in range(SLOTS):
        picked = [s] + [SLOTS + s * ROUNDS + r for r in range(ROUNDS)]
        kept = [means[j] for j in picked] + [squares[j] for j in picked]
        stat[s] = jnp.concatenate(kept + [jnp.zeros((STATS - len(kept), panel), F32)], axis=0)
        for r in range(ROUNDS):
            t = s * ROUNDS + r
            tile[t] = lax.dot_general(
                left[s], right[t], (((0,), (0,)), ((), ())), preferred_element_type=F32
            )
    mine = place[0]
    near = nearer[0]
    here = pl.multiple_of(mine * quarter, quarter)
    across = pl.multiple_of(((mine + 2) % 4) * quarter, quarter)
    base = ROUNDS * quarter
    for slot, targets in ((near, (keep_ref, x_ref)), (1 - near, (half_ref, both_ref))):
        for ref, start in zip(targets, (here, across)):
            for r in range(ROUNDS):
                piece = tile[slot * ROUNDS + r, pl.ds(start, quarter), :]
                ref[pl.ds(r * quarter, quarter), :] = piece.astype(ref.dtype)
            stats = stat[slot]
            if ref.dtype == F32:
                ref[pl.ds(base, STATS), :] = stats
            else:
                high, rest = split_two(stats)
                middle, low = split_two(rest)
                packed = [high, middle, low, jnp.zeros_like(low)]
                ref[pl.ds(base, 4 * STATS), :] = jnp.concatenate(packed, axis=0).astype(BF16)


def finish_kernel(total, place, nearer, keep_ref, x_ref, half_ref, both_ref, out_ref, columns):
    quarter, panel = out_ref.shape[2:]
    base = ROUNDS * quarter
    mine = pl.multiple_of(place[0] * quarter, quarter)
    near = nearer[0]
    sources = ((near, keep_ref, half_ref), (1 - near, x_ref, both_ref))
    for i, (slot, same_ref, other_ref) in enumerate(sources):
        same = same_ref[pl.ds(base, STATS), :]
        parts = other_ref[pl.ds(base, 4 * STATS), :].astype(F32)
        other = parts[2 * STATS : 3 * STATS] + parts[STATS : 2 * STATS] + parts[0:STATS]
        gap = (same - other)[0 : 1 + ROUNDS]
        square = (same + other)[1 + ROUNDS : 2 * (1 + ROUNDS)]
        var = square * (1.0 / total) + (gap * gap) * 0.25
        inv = lax.rsqrt(var + 1e-05)
        pair = jnp.concatenate([gap[0:1], inv[0:1], jnp.zeros((STATS - 2, panel), F32)], axis=0)
        columns[i] = pair.T
        side = columns[i, pl.ds(mine, quarter), :]
        gap_row = side[:, 0:1] * (total / 4)
        inv_row = side[:, 1:2] * total ** (-0.5)
        for r in range(ROUNDS):
            rows = pl.ds(r * quarter, quarter)
            tile = same_ref[rows, :] + other_ref[rows, :].astype(F32)
            tile = tile + gap_row * gap[1 + r : 2 + r]
            out_ref[r, slot] = tile * inv_row * inv[1 + r : 2 + r]


def on_chip(small):
    if not small:
        return jax.ShapeDtypeStruct, lambda value: value
    return pltpu.VMEM, lambda value: pltpu.with_memory_space_constraint(value, pltpu.VMEM)


def shards(expression, assignment, pairing):
    n_wide = lax.axis_size(("half", "rest"))
    n_grp = lax.axis_size(("x", "core"))
    cells, genes = expression.shape
    panels = assignment.shape[0]
    panel = genes // panels
    quarter = panel // n_grp
    total = cells * n_wide * n_grp
    x = lax.axis_index("x")
    place = (x * 2 + lax.axis_index("core")).reshape(1).astype(jnp.int32)
    nearer = (x ^ lax.axis_index("half")).reshape(1).astype(jnp.int32)
    smem = pl.BlockSpec(memory_space=pltpu.SMEM)
    vmem = pl.BlockSpec(memory_space=pltpu.VMEM)
    message = PICKED * cells + SIDE
    received_bytes = 2 * n_wide * message * panel * 2
    array, in_vmem = on_chip(received_bytes <= 4 << 20)
    sent = pl.pallas_call(
        prep_kernel,
        out_shape=array((n_wide, message, panel), BF16),
        in_specs=[smem, smem, vmem],
        out_specs=vmem,
        scratch_shapes=[
            pltpu.VMEM((panels, cells, panel), BF16),
            pltpu.VMEM((panels, panel), F32),
            pltpu.VMEM((panels, panel), F32),
            pltpu.VMEM((SIDE, panel), F32),
        ],
        name="prep",
    )(assignment, pairing, expression)
    here = lax.all_to_all(sent, ("x", "rest"), split_axis=0, concat_axis=0, tiled=True)
    there = lax.ppermute(here, "core", [(0, 1), (1, 0)])
    base = ROUNDS * quarter
    keep, to_x, to_half, to_both = pl.pallas_call(
        functools.partial(gram_kernel, cells),
        out_shape=(
            array((base + STATS, panel), F32),
            array((base + STATS, panel), F32),
            array((base + 4 * STATS, panel), BF16),
            array((base + 4 * STATS, panel), BF16),
        ),
        in_specs=[smem, smem, vmem, vmem],
        out_specs=(vmem, vmem, vmem, vmem),
        scratch_shapes=[
            pltpu.VMEM((SLOTS * ROUNDS, panel, panel), F32),
            pltpu.VMEM((SLOTS, STATS, panel), F32),
        ],
        compiler_params=pltpu.CompilerParams(
            vmem_limit_bytes=min(60 << 20, (8 << 20) + 6 * received_bytes)
        ),
        name="gram",
    )(place, nearer, in_vmem(here), in_vmem(there))
    from_both = lax.ppermute(to_both, ("x", "half"), [(i, i ^ 3) for i in range(4)])
    from_half = lax.ppermute(to_half, "half", [(0, 1), (1, 0)])
    from_x = lax.ppermute(to_x, "x", [(0, 1), (1, 0)])
    return pl.pallas_call(
        functools.partial(finish_kernel, total),
        out_shape=jax.ShapeDtypeStruct((ROUNDS, SLOTS, quarter, panel), F32),
        in_specs=[smem, smem, vmem, vmem, vmem, vmem],
        out_specs=vmem,
        scratch_shapes=[pltpu.VMEM((SLOTS, panel, STATS), F32)],
        name="finish",
    )(place, nearer, in_vmem(keep), in_vmem(from_x), in_vmem(from_half), in_vmem(from_both))


def solution(mesh):
    devices = mesh.devices
    n_wide = devices.shape[1]
    parted = Mesh(devices.reshape(2, 2, 2, n_wide // 2), ("x", "core", "half", "rest"))
    placed = (P(("x", "core", "half", "rest"), None), P(), P())
    return jax.shard_map(
        shards,
        mesh=parted,
        in_specs=placed,
        out_specs=P(None, ("half", "rest"), ("x", "core"), None),
        check_vma=False,
    )
```

```python
import functools

import jax
import jax.numpy as jnp
from jax import lax
from jax.experimental import pallas as pl
from jax.experimental.pallas import tpu as pltpu
from jax.sharding import Mesh
from jax.sharding import PartitionSpec as P


SLOTS = 2
ROUNDS = 2
EACH = 1 + ROUNDS
SIDE = 16
STATS = 8
F32 = jnp.float32
BF16 = jnp.bfloat16


def split_two(value):
    high = value.astype(BF16).astype(F32)
    return high, value - high


def prep_kernel(assignment, pairing, half, x_ref, out_ref, centred, high_rows, low_rows, side):
    cells, genes = x_ref.shape
    panels = assignment.shape[0]
    panel = genes // panels
    n_wide = out_ref.shape[0]

    def one_panel(p, carry):
        start = pl.multiple_of(p * panel, panel)
        block = x_ref[:, pl.ds(start, panel)]
        mean = jnp.sum(block, axis=0, keepdims=True) * (1.0 / cells)
        high, rest = split_two(mean)
        low = rest.astype(BF16).astype(F32)
        centred[p] = (block - (high + low)).astype(BF16)
        high_rows[pl.ds(p, 1), :] = high
        low_rows[pl.ds(p, 1), :] = low
        return carry

    lax.fori_loop(0, panels, one_panel, 0, unroll=panels <= 16)
    side[...] = jnp.zeros_like(side)

    def one_message(w, carry):
        nearer = (w // (n_wide // 2) + half[0]) % 2
        for place, s in ((0, 1 - nearer), (1, nearer)):
            owner = (w + s * (n_wide // 2)) % n_wide
            own = assignment[owner * SLOTS + s]
            for k in range(EACH):
                p = own if k == 0 else pairing[k - 1, own]
                out_ref[w, pl.ds((place * EACH + k) * cells, cells), :] = centred[p]
                side[pl.ds(place * 2 * EACH + k, 1), :] = high_rows[pl.ds(p, 1), :]
                side[pl.ds(place * 2 * EACH + EACH + k, 1), :] = low_rows[pl.ds(p, 1), :]
        out_ref[w, pl.ds(SLOTS * EACH * cells, SIDE), :] = side[...].astype(BF16)
        return carry

    lax.fori_loop(0, n_wide, one_message, 0, unroll=n_wide <= 8)


def gram_kernel(cells, which, place, here_ref, there_ref, same_ref, cross_ref, tile):
    n_wide, _, panel = here_ref.shape
    blocks = 2 * n_wide
    rows = blocks * cells
    quarter = panel // 4

    def part(start, size):
        halves = [r[:, pl.ds(start, size), :].reshape(n_wide * size, panel) for r in (here_ref, there_ref)]
        return jnp.concatenate(halves, axis=0)

    member = lax.broadcasted_iota(jnp.int32, (blocks, rows), 1) // cells
    member = (member == lax.broadcasted_iota(jnp.int32, (blocks, rows), 0)).astype(BF16)
    side = jnp.concatenate(
        [r[:, pl.ds(SLOTS * EACH * cells, SIDE), :].astype(F32) for r in (here_ref, there_ref)], axis=0
    )
    operands, means, squares = [], [], []
    for k in range(EACH):
        data = part((which * EACH + k) * cells, cells)
        sums = jnp.dot(member, data, preferred_element_type=F32)
        row = which * 2 * EACH + k
        block_mean = side[:, row, :] + side[:, row + EACH, :] + sums * (1.0 / cells)
        mean = jnp.sum(block_mean, axis=0, keepdims=True) * (1.0 / blocks)
        shift = block_mean - mean
        wide_data = data.astype(F32)
        square = jnp.sum(wide_data * wide_data, axis=0, keepdims=True) + jnp.sum(
            cells * (shift * shift) - sums * sums * (1.0 / cells), axis=0, keepdims=True
        )
        means.append(mean)
        squares.append(square)
        high, low = split_two(shift)
        scale = cells // 8
        if k == 0:
            extra = [8.0 * high, 8.0 * low, 8.0 * high, sums * 0.125]
        else:
            extra = [scale * high, scale * high, scale * low, sums * (-8.0 / cells)]
        operands.append(jnp.concatenate([data, jnp.concatenate(extra, axis=0).astype(BF16)], axis=0))
    stats = jnp.concatenate(means + squares + [jnp.zeros((STATS - 2 * EACH, panel), F32)], axis=0)
    high, rest = split_two(stats)
    middle, low = split_two(rest)
    packed = jnp.concatenate([high, middle, low, jnp.zeros_like(low)], axis=0).astype(BF16)
    for r in range(ROUNDS):
        tile[r] = lax.dot_general(
            operands[0], operands[1 + r], (((0,), (0,)), ((), ())), preferred_element_type=F32
        )
    mine = place[0]
    base = ROUNDS * quarter
    for ref, index in ((same_ref, mine), (cross_ref, (mine + 2) % 4)):
        start = pl.multiple_of(index * quarter, quarter)
        for r in range(ROUNDS):
            ref[pl.ds(r * quarter, quarter), :] = tile[r, pl.ds(start, quarter), :].astype(ref.dtype)
        if ref.dtype == F32:
            ref[pl.ds(base, STATS), :] = stats
        else:
            ref[pl.ds(base, 4 * STATS), :] = packed


def finish_kernel(total, place, nearer, keep_ref, x_ref, half_ref, both_ref, out_ref, columns):
    quarter, panel = out_ref.shape[2:]
    base = ROUNDS * quarter
    mine = pl.multiple_of(place[0] * quarter, quarter)
    near = nearer[0]
    sources = ((near, keep_ref, half_ref), (1 - near, x_ref, both_ref))
    for i, (slot, same_ref, other_ref) in enumerate(sources):
        same = same_ref[pl.ds(base, STATS), :]
        parts = other_ref[pl.ds(base, 4 * STATS), :].astype(F32)
        other = parts[2 * STATS : 3 * STATS] + parts[STATS : 2 * STATS] + parts[0:STATS]
        gap = (same - other)[0:EACH]
        square = (same + other)[EACH : 2 * EACH]
        var = square * (1.0 / total) + (gap * gap) * 0.25
        inv = lax.rsqrt(var + 1e-05)
        pair = jnp.concatenate([gap[0:1], inv[0:1], jnp.zeros((STATS - 2, panel), F32)], axis=0)
        columns[i] = pair.T
        side = columns[i, pl.ds(mine, quarter), :]
        gap_row = side[:, 0:1] * (total / 4)
        inv_row = side[:, 1:2] * total ** (-0.5)
        for r in range(ROUNDS):
            rows = pl.ds(r * quarter, quarter)
            tile = same_ref[rows, :] + other_ref[rows, :].astype(F32)
            tile = tile + gap_row * gap[1 + r : 2 + r]
            out_ref[r, slot] = tile * inv_row * inv[1 + r : 2 + r]


def on_chip(small):
    if not small:
        return jax.ShapeDtypeStruct, lambda value: value
    return pltpu.VMEM, lambda value: pltpu.with_memory_space_constraint(value, pltpu.VMEM)


def shards(expression, assignment, pairing):
    n_wide = lax.axis_size(("half", "rest"))
    n_grp = lax.axis_size(("x", "core"))
    cells, genes = expression.shape
    panels = assignment.shape[0]
    panel = genes // panels
    quarter = panel // n_grp
    total = cells * n_wide * n_grp
    x = lax.axis_index("x")
    place = (x * 2 + lax.axis_index("core")).reshape(1).astype(jnp.int32)
    nearer = (x ^ lax.axis_index("half")).reshape(1).astype(jnp.int32)
    smem = pl.BlockSpec(memory_space=pltpu.SMEM)
    vmem = pl.BlockSpec(memory_space=pltpu.VMEM)
    message = SLOTS * EACH * cells + SIDE
    received_bytes = 2 * n_wide * message * panel * 2
    array, in_vmem = on_chip(received_bytes <= 4 << 20)
    half = lax.axis_index("half")
    sent = pl.pallas_call(
        prep_kernel,
        out_shape=array((n_wide, message, panel), BF16),
        in_specs=[smem, smem, smem, vmem],
        out_specs=vmem,
        scratch_shapes=[
            pltpu.VMEM((panels, cells, panel), BF16),
            pltpu.VMEM((panels, panel), F32),
            pltpu.VMEM((panels, panel), F32),
            pltpu.VMEM((SIDE, panel), F32),
        ],
        name="prep",
    )(assignment, pairing, half.reshape(1).astype(jnp.int32), expression)
    here = lax.all_to_all(sent, ("x", "rest"), split_axis=0, concat_axis=0, tiled=True)
    there = lax.ppermute(here, "core", [(0, 1), (1, 0)])
    base = ROUNDS * quarter

    def gram(which, rows, dtype):
        return pl.pallas_call(
            functools.partial(gram_kernel, cells, which),
            out_shape=(array((rows, panel), dtype), array((rows, panel), dtype)),
            in_specs=[smem, vmem, vmem],
            out_specs=(vmem, vmem),
            scratch_shapes=[pltpu.VMEM((ROUNDS, panel, panel), F32)],
            compiler_params=pltpu.CompilerParams(
                vmem_limit_bytes=min(60 << 20, (8 << 20) + 6 * received_bytes)
            ),
            name="gram",
        )(place, in_vmem(here), in_vmem(there))

    to_half, to_both = gram(0, base + 4 * STATS, BF16)
    from_both = lax.ppermute(to_both, ("x", "half"), [(i, i ^ 3) for i in range(4)])
    from_half = lax.ppermute(to_half, "half", [(0, 1), (1, 0)])
    keep, to_x = gram(1, base + STATS, F32)
    from_x = lax.ppermute(to_x, "x", [(0, 1), (1, 0)])
    return pl.pallas_call(
        functools.partial(finish_kernel, total),
        out_shape=jax.ShapeDtypeStruct((ROUNDS, SLOTS, quarter, panel), F32),
        in_specs=[smem, smem, vmem, vmem, vmem, vmem],
        out_specs=vmem,
        scratch_shapes=[pltpu.VMEM((SLOTS, panel, STATS), F32)],
        name="finish",
    )(place, nearer, in_vmem(keep), in_vmem(from_x), in_vmem(from_half), in_vmem(from_both))


def solution(mesh):
    devices = mesh.devices
    n_wide = devices.shape[1]
    parted = Mesh(devices.reshape(2, 2, 2, n_wide // 2), ("x", "core", "half", "rest"))
    placed = (P(("x", "core", "half", "rest"), None), P(), P())
    return jax.shard_map(
        shards,
        mesh=parted,
        in_specs=placed,
        out_specs=P(None, ("half", "rest"), ("x", "core"), None),
        check_vma=False,
    )
```

```python
import functools

import jax
import jax.numpy as jnp
from jax import lax
from jax.experimental import pallas as pl
from jax.experimental.pallas import tpu as pltpu
from jax.sharding import Mesh
from jax.sharding import PartitionSpec as P


SLOTS = 2
ROUNDS = 2
EACH = 1 + ROUNDS
SIDE = 16
DIRECT = 8
STATS = 8
F32 = jnp.float32
BF16 = jnp.bfloat16


def split_two(value):
    high = value.astype(BF16).astype(F32)
    return high, value - high


def prep_kernel(apart, assignment, pairing, half, me, x_ref, *refs):
    outs, (centred, high_rows, low_rows, side) = refs[:-4], refs[-4:]
    cells, genes = x_ref.shape
    panels = assignment.shape[0]
    panel = genes // panels
    n_wide = len(outs) if apart else outs[0].shape[0]

    def one_panel(p, carry):
        start = pl.multiple_of(p * panel, panel)
        block = x_ref[:, pl.ds(start, panel)]
        mean = jnp.sum(block, axis=0, keepdims=True) * (1.0 / cells)
        high, rest = split_two(mean)
        low = rest.astype(BF16).astype(F32)
        centred[p] = (block - (high + low)).astype(BF16)
        high_rows[pl.ds(p, 1), :] = high
        low_rows[pl.ds(p, 1), :] = low
        return carry

    lax.fori_loop(0, panels, one_panel, 0, unroll=panels <= 16)
    side[...] = jnp.zeros_like(side)

    def one_message(w, out, at):
        nearer = (w // (n_wide // 2) + half[0]) % 2
        for place, s in ((0, 1 - nearer), (1, nearer)):
            owner = (w + s * (n_wide // 2)) % n_wide
            own = assignment[owner * SLOTS + s]
            for k in range(EACH):
                p = own if k == 0 else pairing[k - 1, own]
                out[at, pl.ds((place * EACH + k) * cells, cells), :] = centred[p]
                side[pl.ds(place * 2 * EACH + k, 1), :] = high_rows[pl.ds(p, 1), :]
                side[pl.ds(place * 2 * EACH + EACH + k, 1), :] = low_rows[pl.ds(p, 1), :]
        out[at, pl.ds(SLOTS * EACH * cells, SIDE), :] = side[...].astype(BF16)

    if apart:
        for k, out in enumerate(outs):
            one_message(me[0] ^ k, out, 0)
    else:
        lax.fori_loop(0, n_wide, lambda w, carry: one_message(w, outs[0], w) or carry, 0)


def gram_kernel(cells, which, place, *refs):
    received, (same_ref, cross_ref, tile) = refs[:-3], refs[-3:]
    panel = same_ref.shape[1]
    blocks = sum(r.shape[0] for r in received)
    rows = blocks * cells
    quarter = panel // 4

    def part(start, size):
        return jnp.concatenate(
            [r[:, pl.ds(start, size), :].reshape(r.shape[0] * size, panel) for r in received], axis=0
        )

    member = lax.broadcasted_iota(jnp.int32, (blocks, rows), 1) // cells
    member = (member == lax.broadcasted_iota(jnp.int32, (blocks, rows), 0)).astype(BF16)
    side = jnp.concatenate(
        [r[:, pl.ds(SLOTS * EACH * cells, SIDE), :].astype(F32) for r in received], axis=0
    )
    operands, means, squares = [], [], []
    for k in range(EACH):
        data = part((which * EACH + k) * cells, cells)
        sums = jnp.dot(member, data, preferred_element_type=F32)
        row = which * 2 * EACH + k
        block_mean = side[:, row, :] + side[:, row + EACH, :] + sums * (1.0 / cells)
        mean = jnp.sum(block_mean, axis=0, keepdims=True) * (1.0 / blocks)
        shift = block_mean - mean
        wide_data = data.astype(F32)
        square = jnp.sum(wide_data * wide_data, axis=0, keepdims=True) + jnp.sum(
            cells * (shift * shift) - sums * sums * (1.0 / cells), axis=0, keepdims=True
        )
        means.append(mean)
        squares.append(square)
        high, low = split_two(shift)
        scale = cells // 8
        if k == 0:
            extra = [8.0 * high, 8.0 * low, 8.0 * high, sums * 0.125]
        else:
            extra = [scale * high, scale * high, scale * low, sums * (-8.0 / cells)]
        operands.append(jnp.concatenate([data, jnp.concatenate(extra, axis=0).astype(BF16)], axis=0))
    stats = jnp.concatenate(means + squares + [jnp.zeros((STATS - 2 * EACH, panel), F32)], axis=0)
    high, rest = split_two(stats)
    middle, low = split_two(rest)
    packed = [high[0 : 2 * EACH], middle[0 : 2 * EACH], low[0:EACH], jnp.zeros((SIDE - 5 * EACH, panel), F32)]
    packed = jnp.concatenate(packed, axis=0).astype(BF16)
    for r in range(ROUNDS):
        tile[r] = lax.dot_general(
            operands[0], operands[1 + r], (((0,), (0,)), ((), ())), preferred_element_type=F32
        )
    mine = place[0]
    base = ROUNDS * quarter
    for ref, index in ((same_ref, mine), (cross_ref, (mine + 2) % 4)):
        start = pl.multiple_of(index * quarter, quarter)
        for r in range(ROUNDS):
            ref[pl.ds(r * quarter, quarter), :] = tile[r, pl.ds(start, quarter), :].astype(ref.dtype)
        if ref.dtype == F32:
            ref[pl.ds(base, STATS), :] = stats
        else:
            ref[pl.ds(base, SIDE), :] = packed


def finish_kernel(total, place, nearer, keep_ref, x_ref, half_ref, both_ref, out_ref, columns):
    quarter, panel = out_ref.shape[2:]
    base = ROUNDS * quarter
    mine = pl.multiple_of(place[0] * quarter, quarter)
    near = nearer[0]
    sources = ((near, keep_ref, half_ref), (1 - near, x_ref, both_ref))
    for i, (slot, same_ref, other_ref) in enumerate(sources):
        same = same_ref[pl.ds(base, STATS), :]
        parts = other_ref[pl.ds(base, SIDE), :].astype(F32)
        other = parts[4 * EACH : 5 * EACH] + parts[2 * EACH : 3 * EACH] + parts[0:EACH]
        gap = same[0:EACH] - other
        square = same[EACH : 2 * EACH] + (parts[3 * EACH : 4 * EACH] + parts[EACH : 2 * EACH])
        var = square * (1.0 / total) + (gap * gap) * 0.25
        inv = lax.rsqrt(var + 1e-05)
        pair = jnp.concatenate([gap[0:1], inv[0:1], jnp.zeros((STATS - 2, panel), F32)], axis=0)
        columns[i] = pair.T
        side = columns[i, pl.ds(mine, quarter), :]
        gap_row = side[:, 0:1] * (total / 4)
        inv_row = side[:, 1:2] * total ** (-0.5)
        for r in range(ROUNDS):
            rows = pl.ds(r * quarter, quarter)
            tile = same_ref[rows, :] + other_ref[rows, :].astype(F32)
            tile = tile + gap_row * gap[1 + r : 2 + r]
            out_ref[r, slot] = tile * inv_row * inv[1 + r : 2 + r]


def on_chip(small):
    if not small:
        return jax.ShapeDtypeStruct, lambda value: value
    return pltpu.VMEM, lambda value: pltpu.with_memory_space_constraint(value, pltpu.VMEM)


def gather(sent, n_wide):
    if len(sent) == 1:
        here = [lax.all_to_all(sent[0], ("x", "rest"), split_axis=0, concat_axis=0, tiled=True)]
    else:
        here = [sent[0]]
        for k in range(1, n_wide):
            here.append(lax.ppermute(sent[k], ("x", "rest"), [(i, i ^ k) for i in range(n_wide)]))
    there = []
    for value in here:
        there.append(lax.ppermute(value, "core", [(0, 1), (1, 0)]))
    return here + there


def shards(expression, assignment, pairing):
    n_wide = lax.axis_size(("half", "rest"))
    n_grp = lax.axis_size(("x", "core"))
    cells, genes = expression.shape
    panels = assignment.shape[0]
    panel = genes // panels
    quarter = panel // n_grp
    total = cells * n_wide * n_grp
    x = lax.axis_index("x")
    place = (x * 2 + lax.axis_index("core")).reshape(1).astype(jnp.int32)
    nearer = (x ^ lax.axis_index("half")).reshape(1).astype(jnp.int32)
    smem = pl.BlockSpec(memory_space=pltpu.SMEM)
    vmem = pl.BlockSpec(memory_space=pltpu.VMEM)
    message = SLOTS * EACH * cells + SIDE
    received_bytes = 2 * n_wide * message * panel * 2
    array, in_vmem = on_chip(received_bytes <= 4 << 20)
    half = lax.axis_index("half").reshape(1).astype(jnp.int32)
    me = lax.axis_index(("x", "rest")).reshape(1).astype(jnp.int32)
    apart = n_wide <= DIRECT
    shape = (1 if apart else n_wide, message, panel)
    sent = pl.pallas_call(
        functools.partial(prep_kernel, apart),
        out_shape=(array(shape, BF16),) * (n_wide if apart else 1),
        in_specs=[smem, smem, smem, smem, vmem],
        out_specs=(vmem,) * (n_wide if apart else 1),
        scratch_shapes=[
            pltpu.VMEM((panels, cells, panel), BF16),
            pltpu.VMEM((panels, panel), F32),
            pltpu.VMEM((panels, panel), F32),
            pltpu.VMEM((SIDE, panel), F32),
        ],
        name="prep",
    )(assignment, pairing, half, me, expression)
    received = gather(sent, n_wide)
    base = ROUNDS * quarter

    def gram(which, rows, dtype):
        return pl.pallas_call(
            functools.partial(gram_kernel, cells, which),
            out_shape=(array((rows, panel), dtype), array((rows, panel), dtype)),
            in_specs=[smem] + [vmem] * len(received),
            out_specs=(vmem, vmem),
            scratch_shapes=[pltpu.VMEM((ROUNDS, panel, panel), F32)],
            compiler_params=pltpu.CompilerParams(
                vmem_limit_bytes=min(60 << 20, (8 << 20) + 6 * received_bytes)
            ),
            name="gram",
        )(place, *map(in_vmem, received))

    to_half, to_both = gram(0, base + SIDE, BF16)
    from_both = lax.ppermute(to_both, ("x", "half"), [(i, i ^ 3) for i in range(4)])
    from_half = lax.ppermute(to_half, "half", [(0, 1), (1, 0)])
    keep, to_x = gram(1, base + STATS, F32)
    from_x = lax.ppermute(to_x, "x", [(0, 1), (1, 0)])
    return pl.pallas_call(
        functools.partial(finish_kernel, total),
        out_shape=jax.ShapeDtypeStruct((ROUNDS, SLOTS, quarter, panel), F32),
        in_specs=[smem, smem, vmem, vmem, vmem, vmem],
        out_specs=vmem,
        scratch_shapes=[pltpu.VMEM((SLOTS, panel, STATS), F32)],
        name="finish",
    )(place, nearer, in_vmem(keep), in_vmem(from_x), in_vmem(from_half), in_vmem(from_both))


def solution(mesh):
    devices = mesh.devices
    n_wide = devices.shape[1]
    parted = Mesh(devices.reshape(2, 2, 2, n_wide // 2), ("x", "core", "half", "rest"))
    placed = (P(("x", "core", "half", "rest"), None), P(), P())
    return jax.shard_map(
        shards,
        mesh=parted,
        in_specs=placed,
        out_specs=P(None, ("half", "rest"), ("x", "core"), None),
        check_vma=False,
    )
```

```python
import functools

import jax
import jax.numpy as jnp
from jax import lax
from jax.experimental import pallas as pl
from jax.experimental.pallas import tpu as pltpu
from jax.sharding import Mesh
from jax.sharding import PartitionSpec as P


SLOTS = 2
ROUNDS = 2
EACH = 1 + ROUNDS
SIDE = 16
DIRECT = 8
ORDER = (0, 7, 5, 6, 3, 4, 2, 1)
STATS = 8
F32 = jnp.float32
BF16 = jnp.bfloat16


def split_two(value):
    high = value.astype(BF16).astype(F32)
    return high, value - high


def prep_kernel(apart, assignment, pairing, half, me, x_ref, *refs):
    outs, (centred, centres, side) = refs[:-3], refs[-3:]
    cells, genes = x_ref.shape
    panels = assignment.shape[0]
    panel = genes // panels
    n_wide = len(outs) if apart else outs[0].shape[0]

    def one_panel(p, carry):
        start = pl.multiple_of(p * panel, panel)
        block = x_ref[:, pl.ds(start, panel)]
        mean = jnp.sum(block, axis=0, keepdims=True) * (1.0 / cells)
        centre = mean.astype(BF16).astype(F32)
        centred[p] = (block - centre).astype(BF16)
        centres[pl.ds(p, 1), :] = centre
        return carry

    lax.fori_loop(0, panels, one_panel, 0, unroll=panels <= 16)
    side[...] = jnp.zeros_like(side)

    def one_message(w, out, at):
        nearer = (w // (n_wide // 2) + half[0]) % 2
        for place, s in ((0, 1 - nearer), (1, nearer)):
            owner = (w + s * (n_wide // 2)) % n_wide
            own = assignment[owner * SLOTS + s]
            for k in range(EACH):
                p = own if k == 0 else pairing[k - 1, own]
                out[at, pl.ds((place * EACH + k) * cells, cells), :] = centred[p]
                side[pl.ds(place * EACH + k, 1), :] = centres[pl.ds(p, 1), :]
        out[at, pl.ds(SLOTS * EACH * cells, STATS), :] = side[...].astype(BF16)

    if apart:
        for k, out in zip(ORDER, outs):
            one_message(me[0] ^ k, out, 0)
    else:
        lax.fori_loop(0, n_wide, lambda w, carry: one_message(w, outs[0], w) or carry, 0)


def gram_kernel(cells, which, place, *refs):
    received, (same_ref, cross_ref, tile) = refs[:-3], refs[-3:]
    panel = same_ref.shape[1]
    blocks = sum(r.shape[0] for r in received)
    rows = blocks * cells
    quarter = panel // 4

    def part(start, size):
        return jnp.concatenate(
            [r[:, pl.ds(start, size), :].reshape(r.shape[0] * size, panel) for r in received], axis=0
        )

    member = lax.broadcasted_iota(jnp.int32, (blocks, rows), 1) // cells
    member = (member == lax.broadcasted_iota(jnp.int32, (blocks, rows), 0)).astype(BF16)
    side = jnp.concatenate(
        [r[:, pl.ds(SLOTS * EACH * cells, STATS), :].astype(F32) for r in received], axis=0
    )
    operands, means, squares = [], [], []
    for k in range(EACH):
        data = part((which * EACH + k) * cells, cells)
        sums = jnp.dot(member, data, preferred_element_type=F32)
        block_mean = side[:, which * EACH + k, :] + sums * (1.0 / cells)
        mean = jnp.sum(block_mean, axis=0, keepdims=True) * (1.0 / blocks)
        shift = block_mean - mean
        wide_data = data.astype(F32)
        square = jnp.sum(wide_data * wide_data, axis=0, keepdims=True) + jnp.sum(
            cells * (shift * shift) - sums * sums * (1.0 / cells), axis=0, keepdims=True
        )
        means.append(mean)
        squares.append(square)
        high, low = split_two(shift)
        scale = cells // 8
        if k == 0:
            extra = [8.0 * high, 8.0 * low, 8.0 * high, sums * 0.125]
        else:
            extra = [scale * high, scale * high, scale * low, sums * (-8.0 / cells)]
        operands.append(jnp.concatenate([data, jnp.concatenate(extra, axis=0).astype(BF16)], axis=0))
    stats = jnp.concatenate(means + squares + [jnp.zeros((STATS - 2 * EACH, panel), F32)], axis=0)
    high, rest = split_two(stats)
    middle, low = split_two(rest)
    packed = [high[0 : 2 * EACH], middle[0 : 2 * EACH], low[0:EACH], jnp.zeros((SIDE - 5 * EACH, panel), F32)]
    packed = jnp.concatenate(packed, axis=0).astype(BF16)
    for r in range(ROUNDS):
        tile[r] = lax.dot_general(
            operands[0], operands[1 + r], (((0,), (0,)), ((), ())), preferred_element_type=F32
        )
    mine = place[0]
    base = ROUNDS * quarter
    for ref, index in ((same_ref, mine), (cross_ref, (mine + 2) % 4)):
        start = pl.multiple_of(index * quarter, quarter)
        for r in range(ROUNDS):
            ref[pl.ds(r * quarter, quarter), :] = tile[r, pl.ds(start, quarter), :].astype(ref.dtype)
        if ref.dtype == F32:
            ref[pl.ds(base, STATS), :] = stats
        else:
            ref[pl.ds(base, SIDE), :] = packed


def unpacked(ref, base):
    if ref.dtype == F32:
        parts = ref[pl.ds(base, STATS), :]
        return parts[0:EACH], parts[EACH : 2 * EACH]
    parts = ref[pl.ds(base, SIDE), :].astype(F32)
    mean = parts[4 * EACH : 5 * EACH] + parts[2 * EACH : 3 * EACH] + parts[0:EACH]
    return mean, parts[3 * EACH : 4 * EACH] + parts[EACH : 2 * EACH]


def finish_kernel(total, place, nearer, keep_ref, x_ref, half_ref, both_ref, out_ref, columns):
    quarter, panel = out_ref.shape[2:]
    base = ROUNDS * quarter
    mine = pl.multiple_of(place[0] * quarter, quarter)
    near = nearer[0]
    sources = ((near, keep_ref, half_ref), (1 - near, x_ref, both_ref))
    for i, (slot, same_ref, other_ref) in enumerate(sources):
        same_mean, same_square = unpacked(same_ref, base)
        other_mean, other_square = unpacked(other_ref, base)
        gap = same_mean - other_mean
        square = same_square + other_square
        var = square * (1.0 / total) + (gap * gap) * 0.25
        inv = lax.rsqrt(var + 1e-05)
        pair = jnp.concatenate([gap[0:1], inv[0:1], jnp.zeros((STATS - 2, panel), F32)], axis=0)
        columns[i] = pair.T
        side = columns[i, pl.ds(mine, quarter), :]
        gap_row = side[:, 0:1] * (total / 4)
        inv_row = side[:, 1:2] * total ** (-0.5)
        for r in range(ROUNDS):
            rows = pl.ds(r * quarter, quarter)
            tile = same_ref[rows, :].astype(F32) + other_ref[rows, :].astype(F32)
            tile = tile + gap_row * gap[1 + r : 2 + r]
            out_ref[r, slot] = tile * inv_row * inv[1 + r : 2 + r]


def on_chip(small):
    if not small:
        return jax.ShapeDtypeStruct, lambda value: value
    return pltpu.VMEM, lambda value: pltpu.with_memory_space_constraint(value, pltpu.VMEM)


def gather(sent, n_wide):
    if len(sent) == 1:
        here = [lax.all_to_all(sent[0], ("x", "rest"), split_axis=0, concat_axis=0, tiled=True)]
    else:
        here = [sent[0]]
        for k, value in zip(ORDER[1:], sent[1:]):
            here.append(lax.ppermute(value, ("x", "rest"), [(i, i ^ k) for i in range(n_wide)]))
    there = []
    for value in here:
        there.append(lax.ppermute(value, "core", [(0, 1), (1, 0)]))
    return here + there


def shards(expression, assignment, pairing):
    n_wide = lax.axis_size(("half", "rest"))
    n_grp = lax.axis_size(("x", "core"))
    cells, genes = expression.shape
    panels = assignment.shape[0]
    panel = genes // panels
    quarter = panel // n_grp
    total = cells * n_wide * n_grp
    x = lax.axis_index("x")
    place = (x * 2 + lax.axis_index("core")).reshape(1).astype(jnp.int32)
    nearer = (x ^ lax.axis_index("half")).reshape(1).astype(jnp.int32)
    smem = pl.BlockSpec(memory_space=pltpu.SMEM)
    vmem = pl.BlockSpec(memory_space=pltpu.VMEM)
    message = SLOTS * EACH * cells + STATS
    received_bytes = 2 * n_wide * message * panel * 2
    array, in_vmem = on_chip(received_bytes <= 4 << 20)
    half = lax.axis_index("half").reshape(1).astype(jnp.int32)
    me = lax.axis_index(("x", "rest")).reshape(1).astype(jnp.int32)
    apart = n_wide <= DIRECT
    shape = (1 if apart else n_wide, message, panel)
    sent = pl.pallas_call(
        functools.partial(prep_kernel, apart),
        out_shape=(array(shape, BF16),) * (n_wide if apart else 1),
        in_specs=[smem, smem, smem, smem, vmem],
        out_specs=(vmem,) * (n_wide if apart else 1),
        scratch_shapes=[
            pltpu.VMEM((panels, cells, panel), BF16),
            pltpu.VMEM((panels, panel), F32),
            pltpu.VMEM((STATS, panel), F32),
        ],
        name="prep",
    )(assignment, pairing, half, me, expression)
    received = gather(sent, n_wide)
    base = ROUNDS * quarter

    def gram(which, side):
        return pl.pallas_call(
            functools.partial(gram_kernel, cells, which),
            out_shape=(array((base + side, panel), BF16 if side == SIDE else F32),) * 2,
            in_specs=[smem] + [vmem] * len(received),
            out_specs=(vmem, vmem),
            scratch_shapes=[pltpu.VMEM((ROUNDS, panel, panel), F32)],
            compiler_params=pltpu.CompilerParams(
                vmem_limit_bytes=min(60 << 20, (8 << 20) + 6 * received_bytes)
            ),
            name="gram",
        )(place, *map(in_vmem, received))

    to_half, to_both = gram(0, SIDE)
    from_both = lax.ppermute(to_both, ("x", "half"), [(i, i ^ 3) for i in range(4)])
    from_half = lax.ppermute(to_half, "half", [(0, 1), (1, 0)])
    keep, to_x = gram(1, STATS)
    from_x = lax.ppermute(to_x, "x", [(0, 1), (1, 0)])
    return pl.pallas_call(
        functools.partial(finish_kernel, total),
        out_shape=jax.ShapeDtypeStruct((ROUNDS, SLOTS, quarter, panel), F32),
        in_specs=[smem, smem, vmem, vmem, vmem, vmem],
        out_specs=vmem,
        scratch_shapes=[pltpu.VMEM((SLOTS, panel, STATS), F32)],
        name="finish",
    )(place, nearer, in_vmem(keep), in_vmem(from_x), in_vmem(from_half), in_vmem(from_both))


def solution(mesh):
    devices = mesh.devices
    n_wide = devices.shape[1]
    parted = Mesh(devices.reshape(2, 2, 2, n_wide // 2), ("x", "core", "half", "rest"))
    placed = (P(("x", "core", "half", "rest"), None), P(), P())
    return jax.shard_map(
        shards,
        mesh=parted,
        in_specs=placed,
        out_specs=P(None, ("half", "rest"), ("x", "core"), None),
        check_vma=False,
    )
```

```python
import functools

import jax
import jax.numpy as jnp
from jax import lax
from jax.experimental import pallas as pl
from jax.experimental.pallas import tpu as pltpu
from jax.sharding import Mesh
from jax.sharding import PartitionSpec as P


SLOTS = 2
ROUNDS = 2
EACH = 1 + ROUNDS
DIRECT = 8
ORDER = (0, 7, 5, 6, 3, 4, 2, 1)
STATS = 8
F32 = jnp.float32
BF16 = jnp.bfloat16


def split_two(value):
    high = value.astype(BF16).astype(F32)
    return high, value - high


def half_turn(row):
    middle = row.shape[1] // 2
    return jnp.concatenate([row[:, middle:], row[:, :middle]], axis=1)


def prep_kernel(apart, assignment, pairing, half, me, x_ref, *refs):
    outs, (centred, centres, side) = refs[:-3], refs[-3:]
    cells, genes = x_ref.shape
    panels = assignment.shape[0]
    panel = genes // panels
    n_wide = len(outs) if apart else outs[0].shape[0]

    def one_panel(p, carry):
        start = pl.multiple_of(p * panel, panel)
        block = x_ref[:, pl.ds(start, panel)]
        mean = jnp.sum(block, axis=0, keepdims=True) * (1.0 / cells)
        centre = mean.astype(BF16).astype(F32)
        centred[p] = (block - centre).astype(BF16)
        centres[pl.ds(p, 1), :] = centre
        return carry

    lax.fori_loop(0, panels, one_panel, 0, unroll=panels <= 16)
    side[...] = jnp.zeros_like(side)

    def one_message(w, out, at):
        nearer = (w // (n_wide // 2) + half[0]) % 2
        for place, s in ((0, 1 - nearer), (1, nearer)):
            owner = (w + s * (n_wide // 2)) % n_wide
            own = assignment[owner * SLOTS + s]
            for k in range(EACH):
                p = own if k == 0 else pairing[k - 1, own]
                out[at, pl.ds((place * EACH + k) * cells, cells), :] = centred[p]
                side[pl.ds(place * EACH + k, 1), :] = centres[pl.ds(p, 1), :]
        out[at, pl.ds(SLOTS * EACH * cells, STATS), :] = side[...].astype(BF16)

    if apart:
        for k, out in zip(ORDER, outs):
            one_message(me[0] ^ k, out, 0)
    else:
        lax.fori_loop(0, n_wide, lambda w, carry: one_message(w, outs[0], w) or carry, 0)


def gram_kernel(cells, which, place, *refs):
    received, (same_ref, cross_ref, tile) = refs[:-3], refs[-3:]
    panel = same_ref.shape[1]
    blocks = sum(r.shape[0] for r in received)
    rows = blocks * cells
    quarter = panel // 4

    def part(start, size):
        return jnp.concatenate(
            [r[:, pl.ds(start, size), :].reshape(r.shape[0] * size, panel) for r in received], axis=0
        )

    member = lax.broadcasted_iota(jnp.int32, (blocks, rows), 1) // cells
    member = (member == lax.broadcasted_iota(jnp.int32, (blocks, rows), 0)).astype(BF16)
    side = jnp.concatenate(
        [r[:, pl.ds(SLOTS * EACH * cells, STATS), :].astype(F32) for r in received], axis=0
    )
    operands, means, squares = [], [], []
    for k in range(EACH):
        data = part((which * EACH + k) * cells, cells)
        sums = jnp.dot(member, data, preferred_element_type=F32)
        block_mean = side[:, which * EACH + k, :] + sums * (1.0 / cells)
        mean = jnp.sum(block_mean, axis=0, keepdims=True) * (1.0 / blocks)
        shift = block_mean - mean
        wide_data = data.astype(F32)
        square = jnp.sum(wide_data * wide_data, axis=0, keepdims=True) + jnp.sum(
            cells * (shift * shift) - sums * sums * (1.0 / cells), axis=0, keepdims=True
        )
        means.append(mean)
        squares.append(square)
        high, low = split_two(shift)
        scale = cells // 8
        if k == 0:
            extra = [8.0 * high, 8.0 * low, 8.0 * high, sums * 0.125]
        else:
            extra = [scale * high, scale * high, scale * low, sums * (-8.0 / cells)]
        operands.append(jnp.concatenate([data, jnp.concatenate(extra, axis=0).astype(BF16)], axis=0))
    stats = jnp.concatenate(means + squares + [jnp.zeros((STATS - 2 * EACH, panel), F32)], axis=0)
    high, low = split_two(stats)
    for r in range(ROUNDS):
        tile[r] = lax.dot_general(
            operands[0], operands[1 + r], (((0,), (0,)), ((), ())), preferred_element_type=F32
        )
    mine = place[0]
    base = ROUNDS * quarter
    for ref, index in ((same_ref, mine), (cross_ref, (mine + 2) % 4)):
        start = pl.multiple_of(index * quarter, quarter)
        for r in range(ROUNDS):
            ref[pl.ds(r * quarter, quarter), :] = tile[r, pl.ds(start, quarter), :].astype(ref.dtype)
        if ref.dtype == F32:
            ref[pl.ds(base, STATS), :] = stats
        else:
            needed = lax.broadcasted_iota(jnp.int32, (1, panel), 1) // quarter == index
            own = [jnp.where(needed, v[0:1], half_turn(v[EACH : EACH + 1])) for v in (high, low)]
            partners = [high[1:EACH], low[1:EACH], high[EACH + 1 : 2 * EACH]]
            ref[pl.ds(base, STATS), :] = jnp.concatenate(own + partners, axis=0).astype(BF16)


def unpacked(ref, base):
    if ref.dtype == F32:
        parts = ref[pl.ds(base, STATS), :]
        return parts[0:EACH], parts[EACH : 2 * EACH]
    parts = ref[pl.ds(base, STATS), :].astype(F32)
    own = parts[0:1] + parts[1:2]
    mean = parts[2 : 2 + ROUNDS] + parts[2 + ROUNDS : 2 + 2 * ROUNDS]
    square = parts[2 + 2 * ROUNDS : 2 + 3 * ROUNDS]
    return jnp.concatenate([own, mean], axis=0), jnp.concatenate([half_turn(own), square], axis=0)


def finish_kernel(total, place, nearer, keep_ref, x_ref, half_ref, both_ref, out_ref, columns):
    quarter, panel = out_ref.shape[2:]
    base = ROUNDS * quarter
    mine = pl.multiple_of(place[0] * quarter, quarter)
    near = nearer[0]
    sources = ((near, keep_ref, half_ref), (1 - near, x_ref, both_ref))
    for i, (slot, same_ref, other_ref) in enumerate(sources):
        same_mean, same_square = unpacked(same_ref, base)
        other_mean, other_square = unpacked(other_ref, base)
        gap = same_mean - other_mean
        square = same_square + other_square
        var = square * (1.0 / total) + (gap * gap) * 0.25
        inv = lax.rsqrt(var + 1e-05)
        pair = jnp.concatenate([gap[0:1], inv[0:1], jnp.zeros((STATS - 2, panel), F32)], axis=0)
        columns[i] = pair.T
        side = columns[i, pl.ds(mine, quarter), :]
        gap_row = side[:, 0:1] * (total / 4)
        inv_row = side[:, 1:2] * total ** (-0.5)
        for r in range(ROUNDS):
            rows = pl.ds(r * quarter, quarter)
            tile = same_ref[rows, :].astype(F32) + other_ref[rows, :].astype(F32)
            tile = tile + gap_row * gap[1 + r : 2 + r]
            out_ref[r, slot] = tile * inv_row * inv[1 + r : 2 + r]


def on_chip(small):
    if not small:
        return jax.ShapeDtypeStruct, lambda value: value
    return pltpu.VMEM, lambda value: pltpu.with_memory_space_constraint(value, pltpu.VMEM)


def gather(sent, n_wide):
    if len(sent) == 1:
        here = [lax.all_to_all(sent[0], ("x", "rest"), split_axis=0, concat_axis=0, tiled=True)]
    else:
        here = [sent[0]]
        for k, value in zip(ORDER[1:], sent[1:]):
            here.append(lax.ppermute(value, ("x", "rest"), [(i, i ^ k) for i in range(n_wide)]))
    there = []
    for value in here:
        there.append(lax.ppermute(value, "core", [(0, 1), (1, 0)]))
    return here + there


def shards(expression, assignment, pairing):
    n_wide = lax.axis_size(("half", "rest"))
    n_grp = lax.axis_size(("x", "core"))
    cells, genes = expression.shape
    panels = assignment.shape[0]
    panel = genes // panels
    quarter = panel // n_grp
    total = cells * n_wide * n_grp
    x = lax.axis_index("x")
    place = (x * 2 + lax.axis_index("core")).reshape(1).astype(jnp.int32)
    nearer = (x ^ lax.axis_index("half")).reshape(1).astype(jnp.int32)
    smem = pl.BlockSpec(memory_space=pltpu.SMEM)
    vmem = pl.BlockSpec(memory_space=pltpu.VMEM)
    message = SLOTS * EACH * cells + STATS
    received_bytes = 2 * n_wide * message * panel * 2
    array, in_vmem = on_chip(received_bytes <= 4 << 20)
    half = lax.axis_index("half").reshape(1).astype(jnp.int32)
    me = lax.axis_index(("x", "rest")).reshape(1).astype(jnp.int32)
    apart = n_wide <= DIRECT
    shape = (1 if apart else n_wide, message, panel)
    sent = pl.pallas_call(
        functools.partial(prep_kernel, apart),
        out_shape=(array(shape, BF16),) * (n_wide if apart else 1),
        in_specs=[smem, smem, smem, smem, vmem],
        out_specs=(vmem,) * (n_wide if apart else 1),
        scratch_shapes=[
            pltpu.VMEM((panels, cells, panel), BF16),
            pltpu.VMEM((panels, panel), F32),
            pltpu.VMEM((STATS, panel), F32),
        ],
        name="prep",
    )(assignment, pairing, half, me, expression)
    received = gather(sent, n_wide)
    base = ROUNDS * quarter

    def gram(which, dtype):
        return pl.pallas_call(
            functools.partial(gram_kernel, cells, which),
            out_shape=(array((base + STATS, panel), dtype),) * 2,
            in_specs=[smem] + [vmem] * len(received),
            out_specs=(vmem, vmem),
            scratch_shapes=[pltpu.VMEM((ROUNDS, panel, panel), F32)],
            compiler_params=pltpu.CompilerParams(
                vmem_limit_bytes=min(60 << 20, (8 << 20) + 6 * received_bytes)
            ),
            name="gram",
        )(place, *map(in_vmem, received))

    to_half, to_both = gram(0, BF16)
    from_both = lax.ppermute(to_both, ("x", "half"), [(i, i ^ 3) for i in range(4)])
    from_half = lax.ppermute(to_half, "half", [(0, 1), (1, 0)])
    keep, to_x = gram(1, F32)
    from_x = lax.ppermute(to_x, "x", [(0, 1), (1, 0)])
    return pl.pallas_call(
        functools.partial(finish_kernel, total),
        out_shape=jax.ShapeDtypeStruct((ROUNDS, SLOTS, quarter, panel), F32),
        in_specs=[smem, smem, vmem, vmem, vmem, vmem],
        out_specs=vmem,
        scratch_shapes=[pltpu.VMEM((SLOTS, panel, STATS), F32)],
        name="finish",
    )(place, nearer, in_vmem(keep), in_vmem(from_x), in_vmem(from_half), in_vmem(from_both))


def solution(mesh):
    devices = mesh.devices
    n_wide = devices.shape[1]
    parted = Mesh(devices.reshape(2, 2, 2, n_wide // 2), ("x", "core", "half", "rest"))
    placed = (P(("x", "core", "half", "rest"), None), P(), P())
    return jax.shard_map(
        shards,
        mesh=parted,
        in_specs=placed,
        out_specs=P(None, ("half", "rest"), ("x", "core"), None),
        check_vma=False,
    )
```

```python
import functools

import jax
import jax.numpy as jnp
from jax import lax
from jax.experimental import pallas as pl
from jax.experimental.pallas import tpu as pltpu
from jax.sharding import Mesh
from jax.sharding import PartitionSpec as P


SLOTS = 2
ROUNDS = 2
EACH = 1 + ROUNDS
DIRECT = 8
ORDER = (0, 7, 5, 6, 3, 4, 2, 1)
STATS = 8
F32 = jnp.float32
BF16 = jnp.bfloat16


def split_two(value):
    high = value.astype(BF16).astype(F32)
    return high, value - high


def half_turn(row):
    middle = row.shape[1] // 2
    return jnp.concatenate([row[:, middle:], row[:, :middle]], axis=1)


def prep_kernel(apart, assignment, pairing, half, me, x_ref, *refs):
    outs, (centred, centres, side) = refs[:-3], refs[-3:]
    cells, genes = x_ref.shape
    panels = assignment.shape[0]
    panel = genes // panels
    n_wide = len(outs) if apart else outs[0].shape[0]

    def one_panel(p, carry):
        start = pl.multiple_of(p * panel, panel)
        block = x_ref[:, pl.ds(start, panel)]
        mean = jnp.sum(block, axis=0, keepdims=True) * (1.0 / cells)
        centre = mean.astype(BF16).astype(F32)
        centred[p] = (block - centre).astype(BF16)
        centres[pl.ds(p, 1), :] = centre
        return carry

    lax.fori_loop(0, panels, one_panel, 0, unroll=panels <= 16)
    side[...] = jnp.zeros_like(side)

    def one_message(w, out, at):
        nearer = (w // (n_wide // 2) + half[0]) % 2
        for place, s in ((0, 1 - nearer), (1, nearer)):
            owner = (w + s * (n_wide // 2)) % n_wide
            own = assignment[owner * SLOTS + s]
            for k in range(EACH):
                p = own if k == 0 else pairing[k - 1, own]
                out[at, pl.ds((place * EACH + k) * cells, cells), :] = centred[p]
                side[pl.ds(place * EACH + k, 1), :] = centres[pl.ds(p, 1), :]
        out[at, pl.ds(SLOTS * EACH * cells, STATS), :] = side[...].astype(BF16)

    if apart:
        for k, out in zip(ORDER, outs):
            one_message(me[0] ^ k, out, 0)
    else:
        lax.fori_loop(0, n_wide, lambda w, carry: one_message(w, outs[0], w) or carry, 0)


def gram_kernel(cells, which, place, *refs):
    received, (same_ref, cross_ref, tile) = refs[:-3], refs[-3:]
    panel = same_ref.shape[1]
    blocks = sum(r.shape[0] for r in received)
    rows = blocks * cells
    quarter = panel // 4

    def part(start, size):
        return jnp.concatenate(
            [r[:, pl.ds(start, size), :].reshape(r.shape[0] * size, panel) for r in received], axis=0
        )

    member = lax.broadcasted_iota(jnp.int32, (blocks, rows), 1) // cells
    member = (member == lax.broadcasted_iota(jnp.int32, (blocks, rows), 0)).astype(BF16)
    side = jnp.concatenate(
        [r[:, pl.ds(SLOTS * EACH * cells, STATS), :].astype(F32) for r in received], axis=0
    )
    operands, means, squares = [], [], []
    for k in range(EACH):
        data = part((which * EACH + k) * cells, cells)
        sums = jnp.dot(member, data, preferred_element_type=F32)
        block_mean = side[:, which * EACH + k, :] + sums * (1.0 / cells)
        mean = jnp.sum(block_mean, axis=0, keepdims=True) * (1.0 / blocks)
        shift = block_mean - mean
        wide_data = data.astype(F32)
        square = jnp.sum(wide_data * wide_data, axis=0, keepdims=True) + jnp.sum(
            cells * (shift * shift) - sums * sums * (1.0 / cells), axis=0, keepdims=True
        )
        means.append(mean)
        squares.append(square)
        high, low = split_two(shift)
        sums_high, sums_low = split_two(sums)
        if k == 0:
            extra = [high, low, high, sums_high, sums_low, sums_high]
        else:
            extra = [cells * v for v in (high, high, low)] + [v * (-1.0 / cells) for v in (sums_high, sums_high, sums_low)]
        operands.append(jnp.concatenate([data, jnp.concatenate(extra, axis=0).astype(BF16)], axis=0))
    stats = jnp.concatenate(means + squares + [jnp.zeros((STATS - 2 * EACH, panel), F32)], axis=0)
    high, low = split_two(stats)
    for r in range(ROUNDS):
        tile[r] = lax.dot_general(
            operands[0], operands[1 + r], (((0,), (0,)), ((), ())), preferred_element_type=F32
        )
    mine = place[0]
    base = ROUNDS * quarter
    for ref, index in ((same_ref, mine), (cross_ref, (mine + 2) % 4)):
        start = pl.multiple_of(index * quarter, quarter)
        for r in range(ROUNDS):
            ref[pl.ds(r * quarter, quarter), :] = tile[r, pl.ds(start, quarter), :].astype(ref.dtype)
        if ref.dtype == F32:
            ref[pl.ds(base, STATS), :] = stats
        else:
            needed = lax.broadcasted_iota(jnp.int32, (1, panel), 1) // quarter == index
            own = [jnp.where(needed, v[0:1], half_turn(v[EACH : EACH + 1])) for v in (high, low)]
            partners = [high[1:EACH], low[1:EACH], high[EACH + 1 : 2 * EACH]]
            ref[pl.ds(base, STATS), :] = jnp.concatenate(own + partners, axis=0).astype(BF16)


def unpacked(ref, base):
    if ref.dtype == F32:
        parts = ref[pl.ds(base, STATS), :]
        return parts[0:EACH], parts[EACH : 2 * EACH]
    parts = ref[pl.ds(base, STATS), :].astype(F32)
    own = parts[0:1] + parts[1:2]
    mean = parts[2 : 2 + ROUNDS] + parts[2 + ROUNDS : 2 + 2 * ROUNDS]
    square = parts[2 + 2 * ROUNDS : 2 + 3 * ROUNDS]
    return jnp.concatenate([own, mean], axis=0), jnp.concatenate([half_turn(own), square], axis=0)


def finish_kernel(total, place, nearer, keep_ref, x_ref, half_ref, both_ref, out_ref, columns):
    quarter, panel = out_ref.shape[2:]
    base = ROUNDS * quarter
    mine = pl.multiple_of(place[0] * quarter, quarter)
    near = nearer[0]
    sources = ((near, keep_ref, half_ref), (1 - near, x_ref, both_ref))
    for i, (slot, same_ref, other_ref) in enumerate(sources):
        same_mean, same_square = unpacked(same_ref, base)
        other_mean, other_square = unpacked(other_ref, base)
        gap = same_mean - other_mean
        square = same_square + other_square
        var = square * (1.0 / total) + (gap * gap) * 0.25
        inv = lax.rsqrt(var + 1e-05)
        pair = jnp.concatenate([gap[0:1], inv[0:1], jnp.zeros((STATS - 2, panel), F32)], axis=0)
        columns[i] = pair.T
        side = columns[i, pl.ds(mine, quarter), :]
        gap_row = side[:, 0:1] * (total / 4)
        inv_row = side[:, 1:2] * total ** (-0.5)
        for r in range(ROUNDS):
            rows = pl.ds(r * quarter, quarter)
            tile = same_ref[rows, :].astype(F32) + other_ref[rows, :].astype(F32)
            tile = tile + gap_row * gap[1 + r : 2 + r]
            out_ref[r, slot] = tile * inv_row * inv[1 + r : 2 + r]


def on_chip(small):
    if not small:
        return jax.ShapeDtypeStruct, lambda value: value
    return pltpu.VMEM, lambda value: pltpu.with_memory_space_constraint(value, pltpu.VMEM)


def gather(sent, n_wide):
    if len(sent) == 1:
        here = [lax.all_to_all(sent[0], ("x", "rest"), split_axis=0, concat_axis=0, tiled=True)]
    else:
        here = [sent[0]]
        for k, value in zip(ORDER[1:], sent[1:]):
            here.append(lax.ppermute(value, ("x", "rest"), [(i, i ^ k) for i in range(n_wide)]))
    there = []
    for value in here:
        there.append(lax.ppermute(value, "core", [(0, 1), (1, 0)]))
    return here + there


def shards(expression, assignment, pairing):
    n_wide = lax.axis_size(("half", "rest"))
    n_grp = lax.axis_size(("x", "core"))
    cells, genes = expression.shape
    panels = assignment.shape[0]
    panel = genes // panels
    quarter = panel // n_grp
    total = cells * n_wide * n_grp
    x = lax.axis_index("x")
    place = (x * 2 + lax.axis_index("core")).reshape(1).astype(jnp.int32)
    nearer = (x ^ lax.axis_index("half")).reshape(1).astype(jnp.int32)
    smem = pl.BlockSpec(memory_space=pltpu.SMEM)
    vmem = pl.BlockSpec(memory_space=pltpu.VMEM)
    message = SLOTS * EACH * cells + STATS
    received_bytes = 2 * n_wide * message * panel * 2
    array, in_vmem = on_chip(received_bytes <= 4 << 20)
    half = lax.axis_index("half").reshape(1).astype(jnp.int32)
    me = lax.axis_index(("x", "rest")).reshape(1).astype(jnp.int32)
    apart = n_wide <= DIRECT
    shape = (1 if apart else n_wide, message, panel)
    sent = pl.pallas_call(
        functools.partial(prep_kernel, apart),
        out_shape=(array(shape, BF16),) * (n_wide if apart else 1),
        in_specs=[smem, smem, smem, smem, vmem],
        out_specs=(vmem,) * (n_wide if apart else 1),
        scratch_shapes=[
            pltpu.VMEM((panels, cells, panel), BF16),
            pltpu.VMEM((panels, panel), F32),
            pltpu.VMEM((STATS, panel), F32),
        ],
        name="prep",
    )(assignment, pairing, half, me, expression)
    received = gather(sent, n_wide)
    base = ROUNDS * quarter

    def gram(which, dtype):
        return pl.pallas_call(
            functools.partial(gram_kernel, cells, which),
            out_shape=(array((base + STATS, panel), dtype),) * 2,
            in_specs=[smem] + [vmem] * len(received),
            out_specs=(vmem, vmem),
            scratch_shapes=[pltpu.VMEM((ROUNDS, panel, panel), F32)],
            compiler_params=pltpu.CompilerParams(
                vmem_limit_bytes=min(60 << 20, (8 << 20) + 6 * received_bytes)
            ),
            name="gram",
        )(place, *map(in_vmem, received))

    to_half, to_both = gram(0, BF16)
    from_both = lax.ppermute(to_both, ("x", "half"), [(i, i ^ 3) for i in range(4)])
    from_half = lax.ppermute(to_half, "half", [(0, 1), (1, 0)])
    keep, to_x = gram(1, F32)
    from_x = lax.ppermute(to_x, "x", [(0, 1), (1, 0)])
    return pl.pallas_call(
        functools.partial(finish_kernel, total),
        out_shape=jax.ShapeDtypeStruct((ROUNDS, SLOTS, quarter, panel), F32),
        in_specs=[smem, smem, vmem, vmem, vmem, vmem],
        out_specs=vmem,
        scratch_shapes=[pltpu.VMEM((SLOTS, panel, STATS), F32)],
        name="finish",
    )(place, nearer, in_vmem(keep), in_vmem(from_x), in_vmem(from_half), in_vmem(from_both))


def solution(mesh):
    devices = mesh.devices
    n_wide = devices.shape[1]
    parted = Mesh(devices.reshape(2, 2, 2, n_wide // 2), ("x", "core", "half", "rest"))
    placed = (P(("x", "core", "half", "rest"), None), P(), P())
    return jax.shard_map(
        shards,
        mesh=parted,
        in_specs=placed,
        out_specs=P(None, ("half", "rest"), ("x", "core"), None),
        check_vma=False,
    )
```

```python
import functools

import jax
import jax.numpy as jnp
from jax import lax
from jax.experimental import pallas as pl
from jax.experimental.pallas import tpu as pltpu
from jax.sharding import Mesh
from jax.sharding import PartitionSpec as P


SLOTS = 2
ROUNDS = 2
EACH = 1 + ROUNDS
DIRECT = 8
ORDER = (0, 7, 5, 6, 3, 4, 2, 1)
STATS = 8
F32 = jnp.float32
BF16 = jnp.bfloat16


def split_two(value):
    high = value.astype(BF16).astype(F32)
    return high, value - high


def half_turn(row):
    middle = row.shape[1] // 2
    return jnp.concatenate([row[:, middle:], row[:, :middle]], axis=1)


def by_core(block):
    middle = block.shape[1] // 2
    first, second = block[:, :middle], block[:, middle:]
    left = lax.broadcasted_iota(jnp.int32, (1, middle), 1) < middle // 2
    return jnp.concatenate(
        [jnp.where(left, first, half_turn(second)), jnp.where(left, half_turn(first), second)], axis=1
    )


def spot(index):
    return index % 2 * 2 + index // 2


def prep_kernel(apart, assignment, pairing, half, me, x_ref, *refs):
    outs, (centred, centres, owned, owned_centres, side) = refs[:-5], refs[-5:]
    cells, genes = x_ref.shape
    panels = assignment.shape[0]
    panel = genes // panels
    n_wide = len(outs) if apart else outs[0].shape[0]

    def one_panel(p, carry):
        start = pl.multiple_of(p * panel, panel)
        block = x_ref[:, pl.ds(start, panel)]
        mean = jnp.sum(block, axis=0, keepdims=True) * (1.0 / cells)
        centre = mean.astype(BF16).astype(F32)
        block = block - centre
        centred[p] = block.astype(BF16)
        centres[pl.ds(p, 1), :] = centre
        owned[p] = by_core(block).astype(BF16)
        owned_centres[pl.ds(p, 1), :] = by_core(centre)
        return carry

    lax.fori_loop(0, panels, one_panel, 0, unroll=panels <= 16)
    side[...] = jnp.zeros_like(side)

    def one_message(w, out, at):
        nearer = (w // (n_wide // 2) + half[0]) % 2
        for place, s in ((0, 1 - nearer), (1, nearer)):
            owner = (w + s * (n_wide // 2)) % n_wide
            own = assignment[owner * SLOTS + s]
            for k in range(EACH):
                p = own if k == 0 else pairing[k - 1, own]
                out[at, pl.ds((place * EACH + k) * cells, cells), :] = (owned if k == 0 else centred)[p]
                side[pl.ds(place * EACH + k, 1), :] = (owned_centres if k == 0 else centres)[pl.ds(p, 1), :]
        out[at, pl.ds(SLOTS * EACH * cells, STATS), :] = side[...].astype(BF16)

    if apart:
        for k, out in zip(ORDER, outs):
            one_message(me[0] ^ k, out, 0)
    else:
        lax.fori_loop(0, n_wide, lambda w, carry: one_message(w, outs[0], w) or carry, 0)


def gram_kernel(cells, which, place, *refs):
    received, (same_ref, cross_ref, tile) = refs[:-3], refs[-3:]
    panel = same_ref.shape[1]
    blocks = sum(r.shape[0] for r in received)
    rows = blocks * cells
    quarter = panel // 4

    def part(start, size):
        return jnp.concatenate(
            [r[:, pl.ds(start, size), :].reshape(r.shape[0] * size, panel) for r in received], axis=0
        )

    member = lax.broadcasted_iota(jnp.int32, (blocks, rows), 1) // cells
    member = (member == lax.broadcasted_iota(jnp.int32, (blocks, rows), 0)).astype(BF16)
    side = jnp.concatenate(
        [r[:, pl.ds(SLOTS * EACH * cells, STATS), :].astype(F32) for r in received], axis=0
    )
    operands, means, squares = [], [], []
    for k in range(EACH):
        data = part((which * EACH + k) * cells, cells)
        sums = jnp.dot(member, data, preferred_element_type=F32)
        block_mean = side[:, which * EACH + k, :] + sums * (1.0 / cells)
        mean = jnp.sum(block_mean, axis=0, keepdims=True) * (1.0 / blocks)
        shift = block_mean - mean
        wide_data = data.astype(F32)
        square = jnp.sum(wide_data * wide_data, axis=0, keepdims=True) + jnp.sum(
            cells * (shift * shift) - sums * sums * (1.0 / cells), axis=0, keepdims=True
        )
        means.append(mean)
        squares.append(square)
        high, low = split_two(shift)
        sums_high, sums_low = split_two(sums)
        if k == 0:
            extra = [high, low, high, sums_high, sums_low, sums_high]
        else:
            extra = [cells * v for v in (high, high, low)] + [v * (-1.0 / cells) for v in (sums_high, sums_high, sums_low)]
        operands.append(jnp.concatenate([data, jnp.concatenate(extra, axis=0).astype(BF16)], axis=0))
    stats = jnp.concatenate(means + squares + [jnp.zeros((STATS - 2 * EACH, panel), F32)], axis=0)
    high, low = split_two(stats)
    mine = place[0]
    own = jnp.where(mine % 2 == 0, operands[0][:, : panel // 2], operands[0][:, panel // 2 :])
    for r in range(ROUNDS):
        tile[r] = lax.dot_general(
            own, operands[1 + r], (((0,), (0,)), ((), ())), preferred_element_type=F32
        )
    base = ROUNDS * quarter
    for ref, index in ((same_ref, mine), (cross_ref, (mine + 2) % 4)):
        start = pl.multiple_of(index // 2 * quarter, quarter)
        for r in range(ROUNDS):
            ref[pl.ds(r * quarter, quarter), :] = tile[r, pl.ds(start, quarter), :].astype(ref.dtype)
        if ref.dtype == F32:
            ref[pl.ds(base, STATS), :] = stats
        else:
            needed = lax.broadcasted_iota(jnp.int32, (1, panel), 1) // quarter == spot(index)
            own = [jnp.where(needed, v[0:1], half_turn(v[EACH : EACH + 1])) for v in (high, low)]
            partners = [high[1:EACH], low[1:EACH], high[EACH + 1 : 2 * EACH]]
            ref[pl.ds(base, STATS), :] = jnp.concatenate(own + partners, axis=0).astype(BF16)


def unpacked(ref, base):
    if ref.dtype == F32:
        parts = ref[pl.ds(base, STATS), :]
        return parts[0:EACH], parts[EACH : 2 * EACH]
    parts = ref[pl.ds(base, STATS), :].astype(F32)
    own = parts[0:1] + parts[1:2]
    mean = parts[2 : 2 + ROUNDS] + parts[2 + ROUNDS : 2 + 2 * ROUNDS]
    square = parts[2 + 2 * ROUNDS : 2 + 3 * ROUNDS]
    return jnp.concatenate([own, mean], axis=0), jnp.concatenate([half_turn(own), square], axis=0)


def finish_kernel(total, place, nearer, keep_ref, x_ref, half_ref, both_ref, out_ref, columns):
    quarter, panel = out_ref.shape[2:]
    base = ROUNDS * quarter
    mine = pl.multiple_of(spot(place[0]) * quarter, quarter)
    near = nearer[0]
    sources = ((near, keep_ref, half_ref), (1 - near, x_ref, both_ref))
    for i, (slot, same_ref, other_ref) in enumerate(sources):
        same_mean, same_square = unpacked(same_ref, base)
        other_mean, other_square = unpacked(other_ref, base)
        gap = same_mean - other_mean
        square = same_square + other_square
        var = square * (1.0 / total) + (gap * gap) * 0.25
        inv = lax.rsqrt(var + 1e-05)
        pair = jnp.concatenate([gap[0:1], inv[0:1], jnp.zeros((STATS - 2, panel), F32)], axis=0)
        columns[i] = pair.T
        side = columns[i, pl.ds(mine, quarter), :]
        gap_row = side[:, 0:1] * (total / 4)
        inv_row = side[:, 1:2] * total ** (-0.5)
        for r in range(ROUNDS):
            rows = pl.ds(r * quarter, quarter)
            tile = same_ref[rows, :].astype(F32) + other_ref[rows, :].astype(F32)
            tile = tile + gap_row * gap[1 + r : 2 + r]
            out_ref[r, slot] = tile * inv_row * inv[1 + r : 2 + r]


def on_chip(small):
    if not small:
        return jax.ShapeDtypeStruct, lambda value: value
    return pltpu.VMEM, lambda value: pltpu.with_memory_space_constraint(value, pltpu.VMEM)


def gather(sent, n_wide):
    if len(sent) == 1:
        here = [lax.all_to_all(sent[0], ("x", "rest"), split_axis=0, concat_axis=0, tiled=True)]
    else:
        here = [sent[0]]
        for k, value in zip(ORDER[1:], sent[1:]):
            here.append(lax.ppermute(value, ("x", "rest"), [(i, i ^ k) for i in range(n_wide)]))
    there = []
    for value in here:
        there.append(lax.ppermute(value, "core", [(0, 1), (1, 0)]))
    return here + there


def shards(expression, assignment, pairing):
    n_wide = lax.axis_size(("half", "rest"))
    n_grp = lax.axis_size(("x", "core"))
    cells, genes = expression.shape
    panels = assignment.shape[0]
    panel = genes // panels
    quarter = panel // n_grp
    total = cells * n_wide * n_grp
    x = lax.axis_index("x")
    place = (x * 2 + lax.axis_index("core")).reshape(1).astype(jnp.int32)
    nearer = (x ^ lax.axis_index("half")).reshape(1).astype(jnp.int32)
    smem = pl.BlockSpec(memory_space=pltpu.SMEM)
    vmem = pl.BlockSpec(memory_space=pltpu.VMEM)
    message = SLOTS * EACH * cells + STATS
    received_bytes = 2 * n_wide * message * panel * 2
    array, in_vmem = on_chip(received_bytes <= 4 << 20)
    half = lax.axis_index("half").reshape(1).astype(jnp.int32)
    me = lax.axis_index(("x", "rest")).reshape(1).astype(jnp.int32)
    apart = n_wide <= DIRECT
    shape = (1 if apart else n_wide, message, panel)
    sent = pl.pallas_call(
        functools.partial(prep_kernel, apart),
        out_shape=(array(shape, BF16),) * (n_wide if apart else 1),
        in_specs=[smem, smem, smem, smem, vmem],
        out_specs=(vmem,) * (n_wide if apart else 1),
        scratch_shapes=[
            pltpu.VMEM((panels, cells, panel), BF16),
            pltpu.VMEM((panels, panel), F32),
            pltpu.VMEM((panels, cells, panel), BF16),
            pltpu.VMEM((panels, panel), F32),
            pltpu.VMEM((STATS, panel), F32),
        ],
        name="prep",
    )(assignment, pairing, half, me, expression)
    received = gather(sent, n_wide)
    base = ROUNDS * quarter

    def gram(which, dtype):
        return pl.pallas_call(
            functools.partial(gram_kernel, cells, which),
            out_shape=(array((base + STATS, panel), dtype),) * 2,
            in_specs=[smem] + [vmem] * len(received),
            out_specs=(vmem, vmem),
            scratch_shapes=[pltpu.VMEM((ROUNDS, panel // 2, panel), F32)],
            compiler_params=pltpu.CompilerParams(
                vmem_limit_bytes=min(60 << 20, (8 << 20) + 6 * received_bytes)
            ),
            name="gram",
        )(place, *map(in_vmem, received))

    to_half, to_both = gram(0, BF16)
    from_both = lax.ppermute(to_both, ("x", "half"), [(i, i ^ 3) for i in range(4)])
    from_half = lax.ppermute(to_half, "half", [(0, 1), (1, 0)])
    keep, to_x = gram(1, F32)
    from_x = lax.ppermute(to_x, "x", [(0, 1), (1, 0)])
    return pl.pallas_call(
        functools.partial(finish_kernel, total),
        out_shape=jax.ShapeDtypeStruct((ROUNDS, SLOTS, quarter, panel), F32),
        in_specs=[smem, smem, vmem, vmem, vmem, vmem],
        out_specs=vmem,
        scratch_shapes=[pltpu.VMEM((SLOTS, panel, STATS), F32)],
        name="finish",
    )(place, nearer, in_vmem(keep), in_vmem(from_x), in_vmem(from_half), in_vmem(from_both))


def solution(mesh):
    devices = mesh.devices
    n_wide = devices.shape[1]
    parted = Mesh(devices.reshape(2, 2, 2, n_wide // 2), ("x", "core", "half", "rest"))
    placed = (P(("x", "core", "half", "rest"), None), P(), P())
    return jax.shard_map(
        shards,
        mesh=parted,
        in_specs=placed,
        out_specs=P(None, ("half", "rest"), ("x", "core"), None),
        check_vma=False,
    )
```

```python
import functools

import jax
import jax.numpy as jnp
from jax import lax
from jax.experimental import pallas as pl
from jax.experimental.pallas import tpu as pltpu
from jax.sharding import Mesh
from jax.sharding import PartitionSpec as P


SLOTS = 2
ROUNDS = 2
EACH = 1 + ROUNDS
DIRECT = 8
ORDERS = ((0, 7, 5, 6, 3, 4, 1, 2), (0, 7, 3, 4, 5, 2, 6, 1))
STATS = 8
F32 = jnp.float32
BF16 = jnp.bfloat16


def split_two(value):
    high = value.astype(BF16).astype(F32)
    return high, value - high


def half_turn(row):
    middle = row.shape[1] // 2
    return jnp.concatenate([row[:, middle:], row[:, :middle]], axis=1)


def prep_kernel(apart, assignment, pairing, half, me, place, x_ref, *refs):
    outs, (centred, centres, side) = refs[:-3], refs[-3:]
    cells, genes = x_ref.shape
    panels = assignment.shape[0]
    panel = genes // panels
    n_wide = len(outs) if apart else outs[0].shape[0]

    def one_panel(p, carry):
        start = pl.multiple_of(p * panel, panel)
        block = x_ref[:, pl.ds(start, panel)]
        mean = jnp.sum(block, axis=0, keepdims=True) * (1.0 / cells)
        centre = mean.astype(BF16).astype(F32)
        centred[p] = (block - centre).astype(BF16)
        centres[pl.ds(p, 1), :] = centre
        return carry

    lax.fori_loop(0, panels, one_panel, 0, unroll=panels <= 16)
    side[...] = jnp.zeros_like(side)

    def one_message(w, out, at):
        nearer = (w // (n_wide // 2) + half[0]) % 2
        for place, s in ((0, 1 - nearer), (1, nearer)):
            owner = (w + s * (n_wide // 2)) % n_wide
            own = assignment[owner * SLOTS + s]
            for k in range(EACH):
                p = own if k == 0 else pairing[k - 1, own]
                out[at, pl.ds((place * EACH + k) * cells, cells), :] = centred[p]
                side[pl.ds(place * EACH + k, 1), :] = centres[pl.ds(p, 1), :]
        out[at, pl.ds(SLOTS * EACH * cells, STATS), :] = side[...].astype(BF16)

    if apart:
        core = half[0]
        for first, second, out in zip(*ORDERS, outs):
            one_message(me[0] ^ (first + core * (second - first)), out, 0)
    else:
        lax.fori_loop(0, n_wide, lambda w, carry: one_message(w, outs[0], w) or carry, 0)


def gram_kernel(cells, which, place, *refs):
    received, (same_ref, cross_ref, tile) = refs[:-3], refs[-3:]
    panel = same_ref.shape[1]
    blocks = sum(r.shape[0] for r in received)
    rows = blocks * cells
    quarter = panel // 4

    def part(start, size):
        return jnp.concatenate(
            [r[:, pl.ds(start, size), :].reshape(r.shape[0] * size, panel) for r in received], axis=0
        )

    member = lax.broadcasted_iota(jnp.int32, (blocks, rows), 1) // cells
    member = (member == lax.broadcasted_iota(jnp.int32, (blocks, rows), 0)).astype(BF16)
    side = jnp.concatenate(
        [r[:, pl.ds(SLOTS * EACH * cells, STATS), :].astype(F32) for r in received], axis=0
    )
    operands, means, squares = [], [], []
    for k in range(EACH):
        data = part((which * EACH + k) * cells, cells)
        sums = jnp.dot(member, data, preferred_element_type=F32)
        block_mean = side[:, which * EACH + k, :] + sums * (1.0 / cells)
        mean = jnp.sum(block_mean, axis=0, keepdims=True) * (1.0 / blocks)
        shift = block_mean - mean
        wide_data = data.astype(F32)
        square = jnp.sum(wide_data * wide_data, axis=0, keepdims=True) + jnp.sum(
            cells * (shift * shift) - sums * sums * (1.0 / cells), axis=0, keepdims=True
        )
        means.append(mean)
        squares.append(square)
        high, low = split_two(shift)
        sums_high, sums_low = split_two(sums)
        if k == 0:
            extra = [high, low, high, sums_high, sums_low, sums_high]
        else:
            extra = [cells * v for v in (high, high, low)] + [v * (-1.0 / cells) for v in (sums_high, sums_high, sums_low)]
        operands.append(jnp.concatenate([data, jnp.concatenate(extra, axis=0).astype(BF16)], axis=0))
    stats = jnp.concatenate(means + squares + [jnp.zeros((STATS - 2 * EACH, panel), F32)], axis=0)
    high, low = split_two(stats)
    for r in range(ROUNDS):
        tile[r] = lax.dot_general(
            operands[0], operands[1 + r], (((0,), (0,)), ((), ())), preferred_element_type=F32
        )
    mine = place[0]
    base = ROUNDS * quarter
    for ref, index in ((same_ref, mine), (cross_ref, (mine + 2) % 4)):
        start = pl.multiple_of(index * quarter, quarter)
        for r in range(ROUNDS):
            ref[pl.ds(r * quarter, quarter), :] = tile[r, pl.ds(start, quarter), :].astype(ref.dtype)
        if ref.dtype == F32:
            ref[pl.ds(base, STATS), :] = stats
        else:
            needed = lax.broadcasted_iota(jnp.int32, (1, panel), 1) // quarter == index
            own = [jnp.where(needed, v[0:1], half_turn(v[EACH : EACH + 1])) for v in (high, low)]
            partners = [high[1:EACH], low[1:EACH], high[EACH + 1 : 2 * EACH]]
            ref[pl.ds(base, STATS), :] = jnp.concatenate(own + partners, axis=0).astype(BF16)


def unpacked(ref, base):
    if ref.dtype == F32:
        parts = ref[pl.ds(base, STATS), :]
        return parts[0:EACH], parts[EACH : 2 * EACH]
    parts = ref[pl.ds(base, STATS), :].astype(F32)
    own = parts[0:1] + parts[1:2]
    mean = parts[2 : 2 + ROUNDS] + parts[2 + ROUNDS : 2 + 2 * ROUNDS]
    square = parts[2 + 2 * ROUNDS : 2 + 3 * ROUNDS]
    return jnp.concatenate([own, mean], axis=0), jnp.concatenate([half_turn(own), square], axis=0)


def finish_kernel(total, place, nearer, keep_ref, x_ref, half_ref, both_ref, out_ref, columns):
    quarter, panel = out_ref.shape[2:]
    base = ROUNDS * quarter
    mine = pl.multiple_of(place[0] * quarter, quarter)
    near = nearer[0]
    sources = ((near, keep_ref, half_ref), (1 - near, x_ref, both_ref))
    for i, (slot, same_ref, other_ref) in enumerate(sources):
        same_mean, same_square = unpacked(same_ref, base)
        other_mean, other_square = unpacked(other_ref, base)
        gap = same_mean - other_mean
        square = same_square + other_square
        var = square * (1.0 / total) + (gap * gap) * 0.25
        inv = lax.rsqrt(var + 1e-05)
        pair = jnp.concatenate([gap[0:1], inv[0:1], jnp.zeros((STATS - 2, panel), F32)], axis=0)
        columns[i] = pair.T
        side = columns[i, pl.ds(mine, quarter), :]
        gap_row = side[:, 0:1] * (total / 4)
        inv_row = side[:, 1:2] * total ** (-0.5)
        for r in range(ROUNDS):
            rows = pl.ds(r * quarter, quarter)
            tile = same_ref[rows, :].astype(F32) + other_ref[rows, :].astype(F32)
            tile = tile + gap_row * gap[1 + r : 2 + r]
            out_ref[r, slot] = tile * inv_row * inv[1 + r : 2 + r]


def on_chip(small):
    if not small:
        return jax.ShapeDtypeStruct, lambda value: value
    return pltpu.VMEM, lambda value: pltpu.with_memory_space_constraint(value, pltpu.VMEM)


def gather(sent, n_wide):
    if len(sent) == 1:
        here = [lax.all_to_all(sent[0], ("x", "rest"), split_axis=0, concat_axis=0, tiled=True)]
    else:
        here = [sent[0]]
        apart = n_wide // 2
        for step in range(1, n_wide):
            pairs = []
            for i in range(2 * n_wide):
                x, core, rest = i // n_wide, i // apart % 2, i % apart
                to = (x * apart + rest) ^ ORDERS[core][step]
                pairs.append((i, (to // apart * 2 + core) * apart + to % apart))
            here.append(lax.ppermute(sent[step], ("x", "half", "rest"), pairs))
    there = []
    for value in here:
        there.append(lax.ppermute(value, "core", [(0, 1), (1, 0)]))
    return here + there


def shards(expression, assignment, pairing):
    n_wide = lax.axis_size(("half", "rest"))
    n_grp = lax.axis_size(("x", "core"))
    cells, genes = expression.shape
    panels = assignment.shape[0]
    panel = genes // panels
    quarter = panel // n_grp
    total = cells * n_wide * n_grp
    x = lax.axis_index("x")
    place = (x * 2 + lax.axis_index("core")).reshape(1).astype(jnp.int32)
    nearer = (x ^ lax.axis_index("half")).reshape(1).astype(jnp.int32)
    smem = pl.BlockSpec(memory_space=pltpu.SMEM)
    vmem = pl.BlockSpec(memory_space=pltpu.VMEM)
    message = SLOTS * EACH * cells + STATS
    received_bytes = 2 * n_wide * message * panel * 2
    array, in_vmem = on_chip(received_bytes <= 4 << 20)
    half = lax.axis_index("half").reshape(1).astype(jnp.int32)
    me = lax.axis_index(("x", "rest")).reshape(1).astype(jnp.int32)
    apart = n_wide <= DIRECT
    shape = (1 if apart else n_wide, message, panel)
    sent = pl.pallas_call(
        functools.partial(prep_kernel, apart),
        out_shape=(array(shape, BF16),) * (n_wide if apart else 1),
        in_specs=[smem, smem, smem, smem, smem, vmem],
        out_specs=(vmem,) * (n_wide if apart else 1),
        scratch_shapes=[
            pltpu.VMEM((panels, cells, panel), BF16),
            pltpu.VMEM((panels, panel), F32),
            pltpu.VMEM((STATS, panel), F32),
        ],
        name="prep",
    )(assignment, pairing, half, me, place, expression)
    received = gather(sent, n_wide)
    base = ROUNDS * quarter

    def gram(which, dtype):
        return pl.pallas_call(
            functools.partial(gram_kernel, cells, which),
            out_shape=(array((base + STATS, panel), dtype),) * 2,
            in_specs=[smem] + [vmem] * len(received),
            out_specs=(vmem, vmem),
            scratch_shapes=[pltpu.VMEM((ROUNDS, panel, panel), F32)],
            compiler_params=pltpu.CompilerParams(
                vmem_limit_bytes=min(60 << 20, (8 << 20) + 6 * received_bytes)
            ),
            name="gram",
        )(place, *map(in_vmem, received))

    to_half, to_both = gram(0, BF16)
    from_both = lax.ppermute(to_both, ("x", "half"), [(i, i ^ 3) for i in range(4)])
    from_half = lax.ppermute(to_half, "half", [(0, 1), (1, 0)])
    keep, to_x = gram(1, F32)
    from_x = lax.ppermute(to_x, "x", [(0, 1), (1, 0)])
    return pl.pallas_call(
        functools.partial(finish_kernel, total),
        out_shape=jax.ShapeDtypeStruct((ROUNDS, SLOTS, quarter, panel), F32),
        in_specs=[smem, smem, vmem, vmem, vmem, vmem],
        out_specs=vmem,
        scratch_shapes=[pltpu.VMEM((SLOTS, panel, STATS), F32)],
        name="finish",
    )(place, nearer, in_vmem(keep), in_vmem(from_x), in_vmem(from_half), in_vmem(from_both))


def solution(mesh):
    devices = mesh.devices
    n_wide = devices.shape[1]
    parted = Mesh(devices.reshape(2, 2, 2, n_wide // 2), ("x", "core", "half", "rest"))
    placed = (P(("x", "core", "half", "rest"), None), P(), P())
    return jax.shard_map(
        shards,
        mesh=parted,
        in_specs=placed,
        out_specs=P(None, ("half", "rest"), ("x", "core"), None),
        check_vma=False,
    )
```
